512 devices in a mesh: seq: 64 (over y, z_lo, core), tensor: 8 (over z_hi, x).
Axes of the slice: x: 4, y: 8, z: 8 (z_hi: 2, z_lo: 4; z = z_hi * 4 + z_lo), core: 2. Of those that a mesh axis runs over, the one named last changes fastest.
Arguments:
- queries: bfloat16 [16384, 3072], P('seq', 'tensor'), may hold values from -100 to 100
- key_tiles: bfloat16 [16384, 3072], P('seq', 'tensor'), may hold values from -6 to 6
- value_tiles: bfloat16 [16384, 3072], P('seq', 'tensor'), may hold values from -6 to 6
- cache_keys: bfloat16 [128, 128, 3072], P('seq', None, 'tensor'), may hold values from -6 to 6
- cache_values: bfloat16 [128, 128, 3072], P('seq', None, 'tensor'), may hold values from -6 to 6
- hidden: bfloat16 [16384, 5120], P('seq', 'tensor'), may hold values from -6 to 6
- out_weight: bfloat16 [3072, 5120], P('seq', 'tensor'), may hold values from -0.21875 to 0.21875
- gate_table: float32 [1000, 5120], P(None, 'tensor'), may hold values from 0.3 to 2.5
- lengths: int32 [16], replicated, may hold values from 512 to 1536, as said below
- page_table: int32 [16, 4], replicated, may hold values from 0 to 127, as said below
- page_count: int32 [16], replicated, may hold values from 0 to 4
- timestep: int32 [16], replicated, may hold values from 0 to 999
Outputs:
- layer_out: bfloat16 [16384, 5120], P('seq', 'tensor')
The draws below stay inside these ranges and needn't reach their ends.
Inputs may be any that keep to these rules, and one draw needn't show every extreme that they name: The lengths sum to 16384. `page_table`: a page named by clip c lies on a seq index that holds some token of clip c (page p lies on seq index p // 2); a page may be named by several clips or twice.
All inputs are finite; a program needn't handle non-finite values.
Results may differ from the reference program's by a relative error of at most 0.018.
Values may be sent and summed in bfloat16 or wider, within the bound.
No kernel may reach another device: no remote copies, remote signals or barrier semaphores. Data moves between devices by JAX's collectives and lax.ppermute only.
A program may use at most 64 MiB of HBM per device.

```python
import math
import jax
import jax.numpy as jnp
from jax import lax

D = 5120
HD = 128
ROWS = 256
LEAST = 512
MOST = 1536
PAGE = 128
POOL = 2
PAGES_CLIP = 4
STEPS = 1000
HQ = 3072
REACH = 6
CLIPS = 16
TOKENS = 16384
N_SEQ = 64


def lengths_helper(key):
    folded = jax.random.fold_in(key, 11)
    first_key, second_key = jax.random.split(folded)
    chosen = jax.random.randint(first_key, (CLIPS // 2,), LEAST, MOST + 1)
    chosen = chosen.at[0].set(MOST)
    paired = jnp.concatenate([chosen, 8 * ROWS - chosen])
    shuffle = jax.random.permutation(second_key, CLIPS)
    return paired[shuffle].astype(jnp.int32)


def draw_lengths(key, part):
    return lengths_helper(key)


def draw_page_table(key, part):
    lengths = lengths_helper(key)
    clip_ends = jnp.cumsum(lengths).astype(jnp.int32)
    clip_starts = clip_ends - lengths
    first_dev = clip_starts // ROWS
    last_dev = (clip_ends - 1) // ROWS
    folded = jax.random.fold_in(key, 12)
    first_key, second_key = jax.random.split(folded)
    offsets = jax.random.randint(first_key, (CLIPS, PAGES_CLIP), 0, 1048576) % (last_dev - first_dev + 1)[:, None]
    owners = first_dev[:, None] + offsets
    slot_ids = jax.random.randint(second_key, (CLIPS, PAGES_CLIP), 0, POOL)
    table = owners * POOL + slot_ids
    column = jnp.arange(PAGES_CLIP)[None, :]
    token_total = 4 * ROWS * CLIPS
    last_page = token_total // ROWS * POOL - 1
    table = jnp.where((clip_ends[:, None] == token_total) & (column == 0), last_page, table)
    table = jnp.where((clip_starts[:, None] == 0) & (column == 1), 0, table)
    return table.astype(jnp.int32)


def draw_page_count(key, part):
    folded = jax.random.fold_in(key, 13)
    counts = jax.random.randint(folded, (CLIPS,), 0, PAGES_CLIP + 1)
    counts = counts.at[0].set(PAGES_CLIP).at[1].set(0)
    return counts.astype(jnp.int32)


def query_key_helper(key):
    folded = jax.random.fold_in(key, 21)
    first_key, second_key = jax.random.split(folded)
    key_draw = jnp.clip(jax.random.normal(first_key, (TOKENS, HQ), jnp.float32), -6.0, 6.0)
    query_draw = 2.0 * jax.random.normal(second_key, (TOKENS, HQ), jnp.float32)
    return (jnp.clip(query_draw, -100.0, 100.0), key_draw)


def draw_queries(key, part):
    return query_key_helper(key)[0].astype(jnp.bfloat16)


def draw_key_tiles(key, part):
    return query_key_helper(key)[1].astype(jnp.bfloat16)


def with_ends(array, key, low, high):
    longest = array.shape.index(max(array.shape))
    spots = []
    for shift in (0, 1):
        where = [jax.random.randint(jax.random.fold_in(key, axis), (), 0, length) for axis, length in enumerate(array.shape)]
        where[longest] = (where[longest] + shift) % array.shape[longest]
        spots.append(tuple(where))
    return array.at[spots[0]].set(low).at[spots[1]].set(high)


def block_scale(stream_key, shape, cuts, smallest, largest):
    gain, own = 1.0, jax.random.fold_in(stream_key, 6)
    for position, parts in cuts:
        heights = jnp.exp(jax.random.uniform(jax.random.fold_in(own, position), (parts,), jnp.float32, smallest / len(cuts), largest / len(cuts)))
        gain = gain * jnp.repeat(heights, shape[position] // parts).reshape([-1 if axis == position else 1 for axis in range(len(shape))])
    return gain


def bell_draw(own_key, extent, scale, most, shards=(), held_as=jnp.bfloat16):
    loudness = block_scale(own_key, extent, shards, -0.22, 0.18) if shards else 1.0
    entries = jax.random.normal(own_key, extent, jnp.float32) * scale * loudness
    return jnp.minimum(jnp.maximum(entries, -most), most).astype(held_as)


def setup_inputs(seed: int = 0) -> dict:
    keys = jax.random.split(jax.random.key(seed), 13)
    return {
        "queries": draw_queries(jax.random.fold_in(keys[12], 71), 0),
        "key_tiles": draw_key_tiles(jax.random.fold_in(keys[12], 71), 0),
        "value_tiles": bell_draw(keys[2], (TOKENS, HQ), 1.0, 6.0, ((0, 64), (1, 8))),
        "cache_keys": bell_draw(keys[3], (N_SEQ * POOL, PAGE, HQ), 1.0, 6.0, ((0, 64), (2, 8))),
        "cache_values": bell_draw(keys[4], (N_SEQ * POOL, PAGE, HQ), 1.0, 6.0, ((0, 64), (2, 8))),
        "hidden": bell_draw(keys[5], (TOKENS, D), 1.0, 6.0, ((0, 64), (1, 8))),
        "out_weight": bell_draw(keys[6], (HQ, D), (HQ // 4) ** -0.5, 0.21875, ((0, 64), (1, 8))),
        "gate_table": jnp.clip(0.3 + 2.2 * jax.random.uniform(keys[7], (STEPS, D), jnp.float32) ** block_scale(keys[7], (STEPS, D), ((1, 8),), -0.2, 0.2), 0.3, 2.5),
        "lengths": draw_lengths(jax.random.fold_in(keys[12], 71), 0),
        "page_table": draw_page_table(jax.random.fold_in(keys[12], 71), 0),
        "page_count": draw_page_count(jax.random.fold_in(keys[12], 71), 0),
        "timestep": with_ends(jax.random.randint(keys[11], (CLIPS,), 0, STEPS), jax.random.fold_in(keys[11], 1), 0, STEPS - 1).astype(jnp.int32),
    }


low_score = -1e+30

def clip_index(positions, clip_ends):
    return lax.optimization_barrier(jnp.sum((positions[:, None] >= clip_ends[None, :]).astype(jnp.int32), axis=1))

def allowed_keys(query_clip, source, clip_ends, page_table, page_count, block_total, row_count):
    key_pos = source * row_count + jnp.arange(row_count, dtype=jnp.int32)
    in_range = (source >= 0) & (source < block_total)
    same_clip = (query_clip[:, None] == clip_index(key_pos, clip_ends)[None, :]) & in_range
    clip_total = clip_ends.shape[0]
    page_ids = source * POOL + jnp.arange(POOL, dtype=jnp.int32)
    live_slots = jnp.arange(page_table.shape[1], dtype=jnp.int32)[None, :] < page_count[:, None]
    named_pages = jnp.any(live_slots[:, :, None] & (page_table[:, :, None] == page_ids[None, None, :]), axis=1)
    member = query_clip[:, None] == jnp.arange(clip_total, dtype=jnp.int32)[None, :]
    page_ok = jnp.any(member[:, :, None] & named_pages[None], axis=1) & in_range
    page_ok = jnp.repeat(page_ok, PAGE, axis=1)
    return jnp.concatenate([same_clip, page_ok], axis=1)

def reference(queries, key_tiles, value_tiles, cache_keys, cache_values, hidden, out_weight, gate_table, lengths, page_table, page_count, timestep):
    token_total = queries.shape[0]
    tile_width = queries.shape[1]
    head_count = tile_width // HD
    block_total = token_total // ROWS
    clip_ends = jnp.cumsum(lengths, dtype=jnp.int32)
    packed_keys = jnp.concatenate([key_tiles.reshape(block_total, ROWS, tile_width), cache_keys.reshape(block_total, POOL * PAGE, tile_width)], axis=1)
    packed_values = jnp.concatenate([value_tiles.reshape(block_total, ROWS, tile_width), cache_values.reshape(block_total, POOL * PAGE, tile_width)], axis=1)
    padded_keys = jnp.pad(packed_keys, ((REACH, REACH), (0, 0), (0, 0)))
    padded_values = jnp.pad(packed_values, ((REACH, REACH), (0, 0), (0, 0)))
    inv_root = 1.0 / math.sqrt(HD)

    def one_block(block_id):
        block_id = block_id.astype(jnp.int32)
        positions = block_id * ROWS + jnp.arange(ROWS, dtype=jnp.int32)
        query_clip = clip_index(positions, clip_ends)
        window_keys = lax.dynamic_slice_in_dim(padded_keys, block_id, 2 * REACH + 1, 0).reshape(-1, head_count, HD)
        window_values = lax.dynamic_slice_in_dim(padded_values, block_id, 2 * REACH + 1, 0).reshape(-1, head_count, HD)
        masks = [allowed_keys(query_clip, block_id - REACH + offset, clip_ends, page_table, page_count, block_total, ROWS) for offset in range(2 * REACH + 1)]
        allowed = jnp.concatenate(masks, axis=1)
        query_rows = lax.dynamic_slice_in_dim(queries, block_id * ROWS, ROWS, 0).reshape(ROWS, head_count, HD)
        scores = jnp.einsum('qhd,khd->hqk', query_rows.astype(jnp.float32), window_keys.astype(jnp.float32)) * inv_root
        scores = jnp.where(allowed[None], scores, low_score)
        top_score = lax.optimization_barrier(jnp.max(scores, axis=2))
        weights = jnp.where(allowed[None], jnp.exp(scores - top_score[:, :, None]), 0.0)
        totals = lax.optimization_barrier(jnp.sum(weights, axis=2))
        rounded = weights.astype(jnp.bfloat16)
        summed = jnp.einsum('hqk,khd->hqd', rounded.astype(jnp.float32), window_values.astype(jnp.float32))
        result = summed / totals[:, :, None]
        return jnp.transpose(result, (1, 0, 2)).reshape(ROWS, tile_width).astype(jnp.bfloat16)
    attention = lax.map(one_block, jnp.arange(block_total, dtype=jnp.int32)).reshape(token_total, tile_width)
    projected = jnp.dot(attention, out_weight, preferred_element_type=jnp.float32)
    token_clip = clip_index(jnp.arange(token_total, dtype=jnp.int32), clip_ends)
    token_gate = gate_table[timestep[token_clip]]
    return (hidden.astype(jnp.float32) + token_gate * projected).astype(jnp.bfloat16)
```

```python
import math

import numpy as np
import jax
import jax.numpy as jnp
from jax import lax
from jax.sharding import Mesh, PartitionSpec as P

HD = 128
PAGE = 128
POOL = 2
REACH = 6

AXES = ("y", "zl", "c", "zh", "x")
SEQ = ("y", "zl", "c")
TENSOR = ("zh", "x")
CHIP = ("y", "zl")

low_score = -1e30


def shifted(block, axes, size, distance, wrap=False):
    if wrap:
        route = [(i, (i + distance) % size) for i in range(size)]
    else:
        route = [(i, i + distance) for i in range(size) if 0 <= i + distance < size]
    return lax.ppermute(block, axes, route)


def swap_cores(block):
    return lax.ppermute(block, "c", [(0, 1), (1, 0)])


def clip_index(positions, clip_ends):
    return jnp.sum((positions[:, None] >= clip_ends[None, :]).astype(jnp.int32), axis=1)


def allowed_keys(query_clip, source, clip_ends, page_table, page_count, block_total, row_count):
    key_pos = source * row_count + jnp.arange(row_count, dtype=jnp.int32)
    in_range = (source >= 0) & (source < block_total)
    same_clip = (query_clip[:, None] == clip_index(key_pos, clip_ends)[None, :]) & in_range
    clip_total = clip_ends.shape[0]
    page_ids = source * POOL + jnp.arange(POOL, dtype=jnp.int32)
    live_slots = jnp.arange(page_table.shape[1], dtype=jnp.int32)[None, :] < page_count[:, None]
    named_pages = jnp.any(
        live_slots[:, :, None] & (page_table[:, :, None] == page_ids[None, None, :]), axis=1
    )
    member = query_clip[:, None] == jnp.arange(clip_total, dtype=jnp.int32)[None, :]
    page_ok = jnp.any(member[:, :, None] & named_pages[None], axis=1) & in_range
    page_ok = jnp.repeat(page_ok, PAGE, axis=1)
    return jnp.concatenate([same_clip, page_ok], axis=1)


def attend(carry_state, query_heads, key_heads, value_heads, allowed):
    running_max, totals, accumulated = carry_state
    scores = jnp.einsum(
        "qhd,khd->hqk", query_heads, key_heads, preferred_element_type=jnp.float32
    ) * (1.0 / math.sqrt(HD))
    scores = jnp.where(allowed[None], scores, low_score)
    new_max = jnp.maximum(running_max, jnp.max(scores, axis=2))
    factor = jnp.exp(running_max - new_max)
    weights = jnp.where(allowed[None], jnp.exp(scores - new_max[:, :, None]), 0.0)
    totals = totals * factor + jnp.sum(weights, axis=2)
    accumulated = accumulated * factor[:, :, None] + jnp.einsum(
        "hqk,khd->hqd",
        weights.astype(jnp.bfloat16),
        value_heads,
        preferred_element_type=jnp.float32,
    )
    return (new_max, totals, accumulated)


def empty_state(head_count, row_count):
    return (
        jnp.full((head_count, row_count), low_score, jnp.float32),
        jnp.zeros((head_count, row_count), jnp.float32),
        jnp.zeros((head_count, row_count, HD), jnp.float32),
    )


def visit_block(carry_state, packed, source, query_heads, query_clip, context):
    clip_ends, page_table, page_count, block_total = context
    row_count = query_heads.shape[0]
    head_count = query_heads.shape[1]
    allowed = allowed_keys(
        query_clip, source, clip_ends, page_table, page_count, block_total, row_count
    )
    key_heads = packed[0].reshape(-1, head_count, HD)
    value_heads = packed[1].reshape(-1, head_count, HD)
    return attend(carry_state, query_heads, key_heads, value_heads, allowed)


def gather_weight(out_weight, sizes, is_first):
    n_y, n_zl = sizes["y"], sizes["zl"]
    rows, cols = out_weight.shape
    other = swap_cores(out_weight)
    pair = jnp.where(
        is_first,
        jnp.concatenate([out_weight, other], axis=0),
        jnp.concatenate([other, out_weight], axis=0),
    )
    zl = lax.axis_index("zl")
    row_block = jnp.zeros((n_zl, 2 * rows, cols), out_weight.dtype)
    row_block = lax.dynamic_update_index_in_dim(row_block, pair, zl, 0)
    for d in range(1, n_zl):
        got = shifted(pair, "zl", n_zl, d, wrap=True)
        row_block = lax.dynamic_update_index_in_dim(row_block, got, (zl - d) % n_zl, 0)
    row_block = row_block.reshape(n_zl * 2 * rows, cols)

    y = lax.axis_index("y")
    full = jnp.zeros((n_y, n_zl * 2 * rows, cols), out_weight.dtype)
    full = lax.dynamic_update_index_in_dim(full, row_block, y, 0)
    below_count = n_y // 2
    above_count = (n_y - 1) // 2
    for j in range(1, below_count + 1):
        route = [(yy * 2, ((yy + j) % n_y) * 2) for yy in range(n_y)]
        if j <= above_count:
            route += [(yy * 2 + 1, ((yy - j) % n_y) * 2 + 1) for yy in range(n_y)]
        got = lax.ppermute(row_block, ("y", "c"), route)
        if j <= above_count:
            traded = swap_cores(got)
            here = jnp.where(is_first, (y - j) % n_y, (y + j) % n_y)
            there = jnp.where(is_first, (y + j) % n_y, (y - j) % n_y)
            full = lax.dynamic_update_index_in_dim(full, got, here, 0)
            full = lax.dynamic_update_index_in_dim(full, traded, there, 0)
        else:
            traded = lax.ppermute(got, "c", [(0, 1)])
            value = jnp.where(is_first, got, traded)
            full = lax.dynamic_update_index_in_dim(full, value, (y - j) % n_y, 0)
    return full.reshape(n_y * n_zl * 2 * rows, cols)


def gather_attention(attention_local, sizes):
    n_x = sizes["x"]
    n_tensor = sizes["zh"] * n_x
    row_count, width = attention_local.shape
    zh = lax.axis_index("zh")
    x = lax.axis_index("x")
    partner = lax.ppermute(attention_local, "zh", [(0, 1), (1, 0)])
    pieces = [(attention_local, zh, x), (partner, 1 - zh, x)]
    for d in range(1, n_x):
        pieces.append((shifted(attention_local, "x", n_x, d, wrap=True), zh, (x - d) % n_x))
        pieces.append((shifted(partner, "x", n_x, d, wrap=True), 1 - zh, (x - d) % n_x))
    full = jnp.zeros((row_count, n_tensor * width), attention_local.dtype)
    for piece, piece_zh, piece_x in pieces:
        start = pl_multiple((piece_zh * n_x + piece_x) * width)
        full = lax.dynamic_update_slice(full, piece, (jnp.int32(0), start))
    return full


def pl_multiple(value):
    return value.astype(jnp.int32)


def make_local(sizes):
    n_chip = sizes["y"] * sizes["zl"]

    def local(
        queries,
        key_tiles,
        value_tiles,
        cache_keys,
        cache_values,
        hidden,
        out_weight,
        gate_table,
        lengths,
        page_table,
        page_count,
        timestep,
    ):
        row_count = queries.shape[0]
        tile_width = queries.shape[1]
        head_count = tile_width // HD
        block_total = n_chip * 2
        chip = lax.axis_index("y") * sizes["zl"] + lax.axis_index("zl")
        core = lax.axis_index("c")
        is_first = core == 0
        seq_index = chip * 2 + core
        clip_ends = jnp.cumsum(lengths, dtype=jnp.int32)
        row_ids = jnp.arange(row_count, dtype=jnp.int32)
        positions = seq_index * row_count + row_ids
        query_clip = clip_index(positions, clip_ends)
        query_heads = queries.reshape(row_count, head_count, HD)
        context = (clip_ends, page_table, page_count, block_total)
        packed = jnp.stack(
            [
                jnp.concatenate([key_tiles, cache_keys.reshape(-1, tile_width)], axis=0),
                jnp.concatenate([value_tiles, cache_values.reshape(-1, tile_width)], axis=0),
            ]
        )
        weight_full = gather_weight(out_weight, sizes, is_first)

        carry_state = visit_block(
            empty_state(head_count, row_count), packed, seq_index, query_heads, query_clip, context
        )
        above = {}
        below = {}
        for d in range(1, 4):
            above[d] = shifted(packed, CHIP, n_chip, -d)
            carry_state = visit_block(
                carry_state, above[d], seq_index + 2 * d, query_heads, query_clip, context
            )
            below[d] = shifted(packed, CHIP, n_chip, d)
            carry_state = visit_block(
                carry_state, below[d], seq_index - 2 * d, query_heads, query_clip, context
            )
        sign = 1 - 2 * core
        outgoing = [
            (packed, 1),
            (jnp.where(is_first, above[1], below[1]), -1),
            (jnp.where(is_first, above[2], below[2]), -3),
            (jnp.where(is_first, above[3], below[3]), -5),
            (jnp.where(is_first, below[1], above[1]), 3),
            (jnp.where(is_first, below[2], above[2]), 5),
        ]
        for block, offset in outgoing:
            got = swap_cores(block)
            carry_state = visit_block(
                carry_state, got, seq_index + sign * offset, query_heads, query_clip, context
            )
        running_max, totals, accumulated = carry_state
        result = accumulated / totals[:, :, None]
        attention_local = (
            jnp.transpose(result, (1, 0, 2)).reshape(row_count, tile_width).astype(jnp.bfloat16)
        )
        attention = gather_attention(attention_local, sizes)
        projected = jnp.dot(attention, weight_full, preferred_element_type=jnp.float32)
        clip_total = lengths.shape[0]
        step_onehot = (
            timestep[:, None] == jnp.arange(gate_table.shape[0], dtype=jnp.int32)[None, :]
        ).astype(jnp.float32)
        clip_gate = jnp.dot(
            step_onehot, gate_table, precision=lax.Precision.HIGHEST, preferred_element_type=jnp.float32
        )
        clip_onehot = (
            query_clip[:, None] == jnp.arange(clip_total, dtype=jnp.int32)[None, :]
        ).astype(jnp.float32)
        token_gate = jnp.dot(
            clip_onehot, clip_gate, precision=lax.Precision.HIGHEST, preferred_element_type=jnp.float32
        )
        return (hidden.astype(jnp.float32) + token_gate * projected).astype(jnp.bfloat16)

    return local


def solution(mesh):
    n_seq = mesh.shape["seq"]
    n_tensor = mesh.shape["tensor"]
    sizes = {"y": n_seq // 8, "zl": 4, "c": 2, "zh": 2, "x": n_tensor // 2}
    devices = np.asarray(mesh.devices).reshape(tuple(sizes[a] for a in AXES))
    fine = Mesh(devices, AXES)
    return jax.shard_map(
        make_local(sizes),
        mesh=fine,
        in_specs=(
            P(SEQ, TENSOR),
            P(SEQ, TENSOR),
            P(SEQ, TENSOR),
            P(SEQ, None, TENSOR),
            P(SEQ, None, TENSOR),
            P(SEQ, TENSOR),
            P(SEQ, TENSOR),
            P(None, TENSOR),
            P(),
            P(),
            P(),
            P(),
        ),
        out_specs=P(SEQ, TENSOR),
        check_vma=False,
    )
```

```python
import math

import numpy as np
import jax
import jax.numpy as jnp
from jax import lax
from jax.sharding import Mesh, PartitionSpec as P

HD = 128
PAGE = 128
POOL = 2
REACH = 6

AXES = ("y", "zl", "c", "zh", "x")
SEQ = ("y", "zl", "c")
TENSOR = ("zh", "x")
CHIP = ("y", "zl")

low_score = -1e30


def shifted(block, axes, size, distance, wrap=False):
    if wrap:
        route = [(i, (i + distance) % size) for i in range(size)]
    else:
        route = [(i, i + distance) for i in range(size) if 0 <= i + distance < size]
    return lax.ppermute(block, axes, route)


def swap_cores(block):
    return lax.ppermute(block, "c", [(0, 1), (1, 0)])


def clip_index(positions, clip_ends):
    return jnp.sum((positions[:, None] >= clip_ends[None, :]).astype(jnp.int32), axis=1)


def allowed_keys(query_clip, source, clip_ends, page_table, page_count, block_total, row_count):
    key_pos = source * row_count + jnp.arange(row_count, dtype=jnp.int32)
    in_range = (source >= 0) & (source < block_total)
    same_clip = (query_clip[:, None] == clip_index(key_pos, clip_ends)[None, :]) & in_range
    clip_total = clip_ends.shape[0]
    page_ids = source * POOL + jnp.arange(POOL, dtype=jnp.int32)
    live_slots = jnp.arange(page_table.shape[1], dtype=jnp.int32)[None, :] < page_count[:, None]
    named_pages = jnp.any(
        live_slots[:, :, None] & (page_table[:, :, None] == page_ids[None, None, :]), axis=1
    )
    member = query_clip[:, None] == jnp.arange(clip_total, dtype=jnp.int32)[None, :]
    page_ok = jnp.any(member[:, :, None] & named_pages[None], axis=1) & in_range
    page_ok = jnp.repeat(page_ok, PAGE, axis=1)
    return jnp.concatenate([same_clip, page_ok], axis=1)


def attend(carry_state, query_heads, key_heads, value_heads, allowed):
    running_max, totals, accumulated = carry_state
    scores = jnp.einsum(
        "qhd,khd->hqk", query_heads, key_heads, preferred_element_type=jnp.float32
    ) * (1.0 / math.sqrt(HD))
    scores = jnp.where(allowed[None], scores, low_score)
    new_max = jnp.maximum(running_max, jnp.max(scores, axis=2))
    factor = jnp.exp(running_max - new_max)
    weights = jnp.where(allowed[None], jnp.exp(scores - new_max[:, :, None]), 0.0)
    totals = totals * factor + jnp.sum(weights, axis=2)
    accumulated = accumulated * factor[:, :, None] + jnp.einsum(
        "hqk,khd->hqd",
        weights.astype(jnp.bfloat16),
        value_heads,
        preferred_element_type=jnp.float32,
    )
    return (new_max, totals, accumulated)


def empty_state(head_count, row_count):
    return (
        jnp.full((head_count, row_count), low_score, jnp.float32),
        jnp.zeros((head_count, row_count), jnp.float32),
        jnp.zeros((head_count, row_count, HD), jnp.float32),
    )


def visit_block(carry_state, packed, source, query_heads, query_clip, context):
    clip_ends, page_table, page_count, block_total = context
    row_count = query_heads.shape[0]
    head_count = query_heads.shape[1]
    allowed = allowed_keys(
        query_clip, source, clip_ends, page_table, page_count, block_total, row_count
    )
    key_heads = packed[0].reshape(-1, head_count, HD)
    value_heads = packed[1].reshape(-1, head_count, HD)
    return attend(carry_state, query_heads, key_heads, value_heads, allowed)


def split_exact(value):
    high = value.astype(jnp.bfloat16)
    rest = value - high.astype(jnp.float32)
    middle = rest.astype(jnp.bfloat16)
    low = (rest - middle.astype(jnp.float32)).astype(jnp.bfloat16)
    return [high, middle, low]


def pack_partial(state):
    running_max, totals, accumulated = state
    head_count, row_count = totals.shape
    safe = jnp.where(totals > 0, totals, 1.0)
    mean = (accumulated / safe[:, :, None]).astype(jnp.bfloat16)
    stats = jnp.stack(split_exact(running_max) + split_exact(totals), axis=1)
    stats = stats.reshape(head_count, 6 * row_count // HD, HD)
    return jnp.concatenate([mean, stats], axis=1)


def unpack_partial(packet, row_count):
    head_count = packet.shape[0]
    mean = packet[:, :row_count].astype(jnp.float32)
    stats = packet[:, row_count:].reshape(head_count, 6, row_count).astype(jnp.float32)
    part_max = (stats[:, 0] + stats[:, 1]) + stats[:, 2]
    part_total = (stats[:, 3] + stats[:, 4]) + stats[:, 5]
    return part_max, part_total, mean


def gather_weight(out_weight, sizes, is_first):
    n_y, n_zl = sizes["y"], sizes["zl"]
    rows, cols = out_weight.shape
    other = swap_cores(out_weight)
    pair = jnp.where(
        is_first,
        jnp.concatenate([out_weight, other], axis=0),
        jnp.concatenate([other, out_weight], axis=0),
    )
    zl = lax.axis_index("zl")
    row_block = jnp.zeros((n_zl, 2 * rows, cols), out_weight.dtype)
    row_block = lax.dynamic_update_index_in_dim(row_block, pair, zl, 0)
    for d in range(1, n_zl):
        got = shifted(pair, "zl", n_zl, d, wrap=True)
        row_block = lax.dynamic_update_index_in_dim(row_block, got, (zl - d) % n_zl, 0)
    row_block = row_block.reshape(n_zl * 2 * rows, cols)

    y = lax.axis_index("y")
    full = jnp.zeros((n_y, n_zl * 2 * rows, cols), out_weight.dtype)
    full = lax.dynamic_update_index_in_dim(full, row_block, y, 0)
    below_count = n_y // 2
    above_count = (n_y - 1) // 2
    for j in range(1, below_count + 1):
        route = [(yy * 2, ((yy + j) % n_y) * 2) for yy in range(n_y)]
        if j <= above_count:
            route += [(yy * 2 + 1, ((yy - j) % n_y) * 2 + 1) for yy in range(n_y)]
        got = lax.ppermute(row_block, ("y", "c"), route)
        if j <= above_count:
            traded = swap_cores(got)
            here = jnp.where(is_first, (y - j) % n_y, (y + j) % n_y)
            there = jnp.where(is_first, (y + j) % n_y, (y - j) % n_y)
            full = lax.dynamic_update_index_in_dim(full, got, here, 0)
            full = lax.dynamic_update_index_in_dim(full, traded, there, 0)
        else:
            traded = lax.ppermute(got, "c", [(0, 1)])
            value = jnp.where(is_first, got, traded)
            full = lax.dynamic_update_index_in_dim(full, value, (y - j) % n_y, 0)
    return full.reshape(n_y * n_zl * 2 * rows, cols)


def gather_attention(attention_local, sizes):
    n_x = sizes["x"]
    n_tensor = sizes["zh"] * n_x
    row_count, width = attention_local.shape
    zh = lax.axis_index("zh")
    x = lax.axis_index("x")
    partner = lax.ppermute(attention_local, "zh", [(0, 1), (1, 0)])
    pieces = [(attention_local, zh, x), (partner, 1 - zh, x)]
    for d in range(1, n_x):
        pieces.append((shifted(attention_local, "x", n_x, d, wrap=True), zh, (x - d) % n_x))
        pieces.append((shifted(partner, "x", n_x, d, wrap=True), 1 - zh, (x - d) % n_x))
    full = jnp.zeros((row_count, n_tensor * width), attention_local.dtype)
    for piece, piece_zh, piece_x in pieces:
        start = pl_multiple((piece_zh * n_x + piece_x) * width)
        full = lax.dynamic_update_slice(full, piece, (jnp.int32(0), start))
    return full


def pl_multiple(value):
    return value.astype(jnp.int32)


def make_local(sizes):
    n_chip = sizes["y"] * sizes["zl"]

    def local(
        queries,
        key_tiles,
        value_tiles,
        cache_keys,
        cache_values,
        hidden,
        out_weight,
        gate_table,
        lengths,
        page_table,
        page_count,
        timestep,
    ):
        row_count = queries.shape[0]
        tile_width = queries.shape[1]
        head_count = tile_width // HD
        block_total = n_chip * 2
        chip = lax.axis_index("y") * sizes["zl"] + lax.axis_index("zl")
        core = lax.axis_index("c")
        is_first = core == 0
        seq_index = chip * 2 + core
        clip_ends = jnp.cumsum(lengths, dtype=jnp.int32)
        row_ids = jnp.arange(row_count, dtype=jnp.int32)
        positions = seq_index * row_count + row_ids
        query_clip = clip_index(positions, clip_ends)
        query_heads = queries.reshape(row_count, head_count, HD)
        context = (clip_ends, page_table, page_count, block_total)
        packed = jnp.stack(
            [
                jnp.concatenate([key_tiles, cache_keys.reshape(-1, tile_width)], axis=0),
                jnp.concatenate([value_tiles, cache_values.reshape(-1, tile_width)], axis=0),
            ]
        )
        weight_full = gather_weight(out_weight, sizes, is_first)

        partner_kv = swap_cores(packed)
        sign = 1 - 2 * core

        def partial_for(q_heads, q_seq):
            q_clip = clip_index(q_seq * row_count + row_ids, clip_ends)
            state = visit_block(
                empty_state(head_count, row_count), packed, seq_index, q_heads, q_clip, context
            )
            return visit_block(state, partner_kv, seq_index + sign, q_heads, q_clip, context)

        own_max, own_total, own_acc = partial_for(query_heads, seq_index)
        returned = []
        for d in range(1, 4):
            for direction in (1, -1):
                visitor = shifted(queries, CHIP, n_chip, -direction * d)
                state = partial_for(
                    visitor.reshape(row_count, head_count, HD), seq_index + 2 * direction * d
                )
                back = shifted(pack_partial(state), CHIP, n_chip, direction * d)
                returned.append(unpack_partial(back, row_count))
        top = own_max
        for part_max, part_total, _ in returned:
            top = jnp.maximum(top, jnp.where(part_total > 0, part_max, low_score))
        own_scale = jnp.exp(own_max - top)
        totals = own_total * own_scale
        accumulated = own_acc * own_scale[:, :, None]
        for part_max, part_total, part_mean in returned:
            scale = jnp.where(part_total > 0, part_total * jnp.exp(part_max - top), 0.0)
            totals = totals + scale
            accumulated = accumulated + part_mean * scale[:, :, None]
        result = accumulated / totals[:, :, None]
        attention_local = (
            jnp.transpose(result, (1, 0, 2)).reshape(row_count, tile_width).astype(jnp.bfloat16)
        )
        attention = gather_attention(attention_local, sizes)
        projected = jnp.dot(attention, weight_full, preferred_element_type=jnp.float32)
        clip_total = lengths.shape[0]
        step_onehot = (
            timestep[:, None] == jnp.arange(gate_table.shape[0], dtype=jnp.int32)[None, :]
        ).astype(jnp.float32)
        clip_gate = jnp.dot(
            step_onehot, gate_table, precision=lax.Precision.HIGHEST, preferred_element_type=jnp.float32
        )
        clip_onehot = (
            query_clip[:, None] == jnp.arange(clip_total, dtype=jnp.int32)[None, :]
        ).astype(jnp.float32)
        token_gate = jnp.dot(
            clip_onehot, clip_gate, precision=lax.Precision.HIGHEST, preferred_element_type=jnp.float32
        )
        return (hidden.astype(jnp.float32) + token_gate * projected).astype(jnp.bfloat16)

    return local


def solution(mesh):
    n_seq = mesh.shape["seq"]
    n_tensor = mesh.shape["tensor"]
    sizes = {"y": n_seq // 8, "zl": 4, "c": 2, "zh": 2, "x": n_tensor // 2}
    devices = np.asarray(mesh.devices).reshape(tuple(sizes[a] for a in AXES))
    fine = Mesh(devices, AXES)
    return jax.shard_map(
        make_local(sizes),
        mesh=fine,
        in_specs=(
            P(SEQ, TENSOR),
            P(SEQ, TENSOR),
            P(SEQ, TENSOR),
            P(SEQ, None, TENSOR),
            P(SEQ, None, TENSOR),
            P(SEQ, TENSOR),
            P(SEQ, TENSOR),
            P(None, TENSOR),
            P(),
            P(),
            P(),
            P(),
        ),
        out_specs=P(SEQ, TENSOR),
        check_vma=False,
    )
```

```python
import math

import numpy as np
import jax
import jax.numpy as jnp
from jax import lax
from jax.sharding import Mesh, PartitionSpec as P

HD = 128
PAGE = 128
POOL = 2
REACH = 6

AXES = ("y", "zl", "c", "zh", "x")
SEQ = ("y", "zl", "c")
TENSOR = ("zh", "x")
CHIP = ("y", "zl")

low_score = -1e30


def shifted(block, axes, size, distance, wrap=False):
    if wrap:
        route = [(i, (i + distance) % size) for i in range(size)]
    else:
        route = [(i, i + distance) for i in range(size) if 0 <= i + distance < size]
    return lax.ppermute(block, axes, route)


def swap_cores(block):
    return lax.ppermute(block, "c", [(0, 1), (1, 0)])


def clip_index(positions, clip_ends):
    return jnp.sum((positions[:, None] >= clip_ends[None, :]).astype(jnp.int32), axis=1)


def allowed_keys(query_clip, source, clip_ends, page_table, page_count, block_total, row_count):
    key_pos = source * row_count + jnp.arange(row_count, dtype=jnp.int32)
    in_range = (source >= 0) & (source < block_total)
    same_clip = (query_clip[:, None] == clip_index(key_pos, clip_ends)[None, :]) & in_range
    clip_total = clip_ends.shape[0]
    page_ids = source * POOL + jnp.arange(POOL, dtype=jnp.int32)
    live_slots = jnp.arange(page_table.shape[1], dtype=jnp.int32)[None, :] < page_count[:, None]
    named_pages = jnp.any(
        live_slots[:, :, None] & (page_table[:, :, None] == page_ids[None, None, :]), axis=1
    )
    member = query_clip[:, None] == jnp.arange(clip_total, dtype=jnp.int32)[None, :]
    page_ok = jnp.any(member[:, :, None] & named_pages[None], axis=1) & in_range
    page_ok = jnp.repeat(page_ok, PAGE, axis=1)
    return jnp.concatenate([same_clip, page_ok], axis=1)


def attend(carry_state, query_heads, key_heads, value_heads, allowed):
    running_max, totals, accumulated = carry_state
    scores = jnp.einsum(
        "qhd,khd->hqk", query_heads, key_heads, preferred_element_type=jnp.float32
    ) * (1.0 / math.sqrt(HD))
    scores = jnp.where(allowed[None], scores, low_score)
    new_max = jnp.maximum(running_max, jnp.max(scores, axis=2))
    factor = jnp.exp(running_max - new_max)
    weights = jnp.where(allowed[None], jnp.exp(scores - new_max[:, :, None]), 0.0)
    totals = totals * factor + jnp.sum(weights, axis=2)
    accumulated = accumulated * factor[:, :, None] + jnp.einsum(
        "hqk,khd->hqd",
        weights.astype(jnp.bfloat16),
        value_heads,
        preferred_element_type=jnp.float32,
    )
    return (new_max, totals, accumulated)


def empty_state(head_count, row_count):
    return (
        jnp.full((head_count, row_count), low_score, jnp.float32),
        jnp.zeros((head_count, row_count), jnp.float32),
        jnp.zeros((head_count, row_count, HD), jnp.float32),
    )


def visit_block(carry_state, packed, source, query_heads, query_clip, context):
    clip_ends, page_table, page_count, block_total = context
    row_count = query_heads.shape[0]
    head_count = query_heads.shape[1]
    allowed = allowed_keys(
        query_clip, source, clip_ends, page_table, page_count, block_total, row_count
    )
    key_heads = packed[0].reshape(-1, head_count, HD)
    value_heads = packed[1].reshape(-1, head_count, HD)
    return attend(carry_state, query_heads, key_heads, value_heads, allowed)


def split_exact(value):
    high = value.astype(jnp.bfloat16)
    rest = value - high.astype(jnp.float32)
    middle = rest.astype(jnp.bfloat16)
    low = (rest - middle.astype(jnp.float32)).astype(jnp.bfloat16)
    return [high, middle, low]


def pack_partial(state):
    running_max, totals, accumulated = state
    head_count, row_count = totals.shape
    safe = jnp.where(totals > 0, totals, 1.0)
    mean = (accumulated / safe[:, :, None]).astype(jnp.bfloat16)
    stats = jnp.stack(split_exact(running_max) + split_exact(totals), axis=1)
    stats = stats.reshape(head_count, 6 * row_count // HD, HD)
    return jnp.concatenate([mean, stats], axis=1)


def unpack_partial(packet, row_count):
    head_count = packet.shape[0]
    mean = packet[:, :row_count].astype(jnp.float32)
    stats = packet[:, row_count:].reshape(head_count, 6, row_count).astype(jnp.float32)
    part_max = (stats[:, 0] + stats[:, 1]) + stats[:, 2]
    part_total = (stats[:, 3] + stats[:, 4]) + stats[:, 5]
    return part_max, part_total, mean


def combine_parts(parts):
    top = jnp.full_like(parts[0][0], low_score)
    for part_max, part_total, _ in parts:
        top = jnp.maximum(top, jnp.where(part_total > 0, part_max, low_score))
    totals = jnp.zeros_like(top)
    accumulated = jnp.zeros_like(parts[0][2])
    for part_max, part_total, part_mean in parts:
        scale = jnp.where(part_total > 0, part_total * jnp.exp(part_max - top), 0.0)
        totals = totals + scale
        accumulated = accumulated + part_mean * scale[:, :, None]
    mean = accumulated / jnp.where(totals > 0, totals, 1.0)[:, :, None]
    return (top, totals, mean)


def gather_weight(out_weight, sizes, is_first):
    n_y, n_zl = sizes["y"], sizes["zl"]
    rows, cols = out_weight.shape
    other = swap_cores(out_weight)
    pair = jnp.where(
        is_first,
        jnp.concatenate([out_weight, other], axis=0),
        jnp.concatenate([other, out_weight], axis=0),
    )
    zl = lax.axis_index("zl")
    row_block = jnp.zeros((n_zl, 2 * rows, cols), out_weight.dtype)
    row_block = lax.dynamic_update_index_in_dim(row_block, pair, zl, 0)
    for d in range(1, n_zl):
        got = shifted(pair, "zl", n_zl, d, wrap=True)
        row_block = lax.dynamic_update_index_in_dim(row_block, got, (zl - d) % n_zl, 0)
    row_block = row_block.reshape(n_zl * 2 * rows, cols)

    y = lax.axis_index("y")
    full = jnp.zeros((n_y, n_zl * 2 * rows, cols), out_weight.dtype)
    full = lax.dynamic_update_index_in_dim(full, row_block, y, 0)
    below_count = n_y // 2
    above_count = (n_y - 1) // 2
    received = []
    for j in range(1, below_count + 1):
        route = [(yy * 2, ((yy + j) % n_y) * 2) for yy in range(n_y)]
        if j <= above_count:
            route += [(yy * 2 + 1, ((yy - j) % n_y) * 2 + 1) for yy in range(n_y)]
        received.append(lax.ppermute(row_block, ("y", "c"), route))
    traded = swap_cores(jnp.stack(received))
    for j in range(1, below_count + 1):
        got = received[j - 1]
        if j <= above_count:
            here = jnp.where(is_first, (y - j) % n_y, (y + j) % n_y)
            there = jnp.where(is_first, (y + j) % n_y, (y - j) % n_y)
            full = lax.dynamic_update_index_in_dim(full, got, here, 0)
            full = lax.dynamic_update_index_in_dim(full, traded[j - 1], there, 0)
        else:
            value = jnp.where(is_first, got, traded[j - 1])
            full = lax.dynamic_update_index_in_dim(full, value, (y - j) % n_y, 0)
    return full.reshape(n_y * n_zl * 2 * rows, cols)


def gather_attention(attention_local, sizes):
    n_x = sizes["x"]
    n_tensor = sizes["zh"] * n_x
    row_count, width = attention_local.shape
    zh = lax.axis_index("zh")
    x = lax.axis_index("x")
    partner = lax.ppermute(attention_local, "zh", [(0, 1), (1, 0)])
    both = jnp.where(
        zh == 0,
        jnp.concatenate([attention_local, partner], axis=1),
        jnp.concatenate([partner, attention_local], axis=1),
    )
    pieces = [(both, x)]
    for d in range(1, n_x):
        pieces.append((shifted(both, "x", n_x, d, wrap=True), (x - d) % n_x))
    full = jnp.zeros((row_count, n_tensor * width), attention_local.dtype)
    for piece, piece_x in pieces:
        for half in range(2):
            start = pl_multiple((half * n_x + piece_x) * width)
            full = lax.dynamic_update_slice(
                full, piece[:, half * width:(half + 1) * width], (jnp.int32(0), start)
            )
    return full


def pl_multiple(value):
    return value.astype(jnp.int32)


def make_local(sizes):
    n_chip = sizes["y"] * sizes["zl"]

    def local(
        queries,
        key_tiles,
        value_tiles,
        cache_keys,
        cache_values,
        hidden,
        out_weight,
        gate_table,
        lengths,
        page_table,
        page_count,
        timestep,
    ):
        row_count = queries.shape[0]
        tile_width = queries.shape[1]
        head_count = tile_width // HD
        block_total = n_chip * 2
        chip = lax.axis_index("y") * sizes["zl"] + lax.axis_index("zl")
        core = lax.axis_index("c")
        is_first = core == 0
        seq_index = chip * 2 + core
        clip_ends = jnp.cumsum(lengths, dtype=jnp.int32)
        row_ids = jnp.arange(row_count, dtype=jnp.int32)
        positions = seq_index * row_count + row_ids
        query_clip = clip_index(positions, clip_ends)
        query_heads = queries.reshape(row_count, head_count, HD)
        context = (clip_ends, page_table, page_count, block_total)
        packed = jnp.stack(
            [
                jnp.concatenate([key_tiles, cache_keys.reshape(-1, tile_width)], axis=0),
                jnp.concatenate([value_tiles, cache_values.reshape(-1, tile_width)], axis=0),
            ]
        )
        weight_full = gather_weight(out_weight, sizes, is_first)

        partner_kv = swap_cores(packed)
        partner_q = swap_cores(queries)
        sign = 1 - 2 * core
        pair = jnp.where(
            is_first, jnp.stack([queries, partner_q]), jnp.stack([partner_q, queries])
        )

        def partial_for(q_heads, q_seq):
            q_clip = clip_index(q_seq * row_count + row_ids, clip_ends)
            state = visit_block(
                empty_state(head_count, row_count), packed, seq_index, q_heads, q_clip, context
            )
            return visit_block(state, partner_kv, seq_index + sign, q_heads, q_clip, context)

        own_max, own_total, own_acc = partial_for(query_heads, seq_index)
        own_part = (own_max, own_total, own_acc / jnp.where(own_total > 0, own_total, 1.0)[:, :, None])
        n_seq = n_chip * 2
        returned = [[], []]
        for d in range(1, 4):
            out_route = [(i * 2, (i + d) * 2) for i in range(n_chip) if i + d < n_chip]
            out_route += [(i * 2 + 1, (i - d) * 2 + 1) for i in range(n_chip) if i - d >= 0]
            visitors = lax.ppermute(pair, SEQ, out_route)
            visitor_chip = chip - sign * d
            packets = []
            for j in range(2):
                state = partial_for(
                    visitors[j].reshape(row_count, head_count, HD), visitor_chip * 2 + j
                )
                packets.append(pack_partial(state))
            back_route = [(b, a) for a, b in out_route]
            back = lax.ppermute(jnp.stack(packets), SEQ, back_route)
            for j in range(2):
                returned[j].append(unpack_partial(back[j], row_count))
        combined = [combine_parts(returned[j]) for j in range(2)]
        mine = [jnp.where(is_first, a, b) for a, b in zip(combined[0], combined[1])]
        theirs = [jnp.where(is_first, b, a) for a, b in zip(combined[0], combined[1])]
        sent = jnp.concatenate(
            [theirs[2], jnp.stack([theirs[0], theirs[1]], axis=1).reshape(head_count, 4, HD)],
            axis=1,
        )
        got = swap_cores(sent)
        got_stats = got[:, row_count:].reshape(head_count, 2, row_count)
        from_partner = (got_stats[:, 0], got_stats[:, 1], got[:, :row_count])
        _, _, result = combine_parts([own_part, tuple(mine), from_partner])
        attention_local = (
            jnp.transpose(result, (1, 0, 2)).reshape(row_count, tile_width).astype(jnp.bfloat16)
        )
        attention = gather_attention(attention_local, sizes)
        projected = jnp.dot(attention, weight_full, preferred_element_type=jnp.float32)
        clip_total = lengths.shape[0]
        step_onehot = (
            timestep[:, None] == jnp.arange(gate_table.shape[0], dtype=jnp.int32)[None, :]
        ).astype(jnp.float32)
        clip_gate = jnp.dot(
            step_onehot, gate_table, precision=lax.Precision.HIGHEST, preferred_element_type=jnp.float32
        )
        clip_onehot = (
            query_clip[:, None] == jnp.arange(clip_total, dtype=jnp.int32)[None, :]
        ).astype(jnp.float32)
        token_gate = jnp.dot(
            clip_onehot, clip_gate, precision=lax.Precision.HIGHEST, preferred_element_type=jnp.float32
        )
        return (hidden.astype(jnp.float32) + token_gate * projected).astype(jnp.bfloat16)

    return local


def solution(mesh):
    n_seq = mesh.shape["seq"]
    n_tensor = mesh.shape["tensor"]
    sizes = {"y": n_seq // 8, "zl": 4, "c": 2, "zh": 2, "x": n_tensor // 2}
    devices = np.asarray(mesh.devices).reshape(tuple(sizes[a] for a in AXES))
    fine = Mesh(devices, AXES)
    return jax.shard_map(
        make_local(sizes),
        mesh=fine,
        in_specs=(
            P(SEQ, TENSOR),
            P(SEQ, TENSOR),
            P(SEQ, TENSOR),
            P(SEQ, None, TENSOR),
            P(SEQ, None, TENSOR),
            P(SEQ, TENSOR),
            P(SEQ, TENSOR),
            P(None, TENSOR),
            P(),
            P(),
            P(),
            P(),
        ),
        out_specs=P(SEQ, TENSOR),
        check_vma=False,
    )
```

```python
import math

import numpy as np
import jax
import jax.numpy as jnp
from jax import lax
from jax.sharding import Mesh, PartitionSpec as P

HD = 128
PAGE = 128
POOL = 2
REACH = 6

AXES = ("y", "zl", "c", "zh", "x")
SEQ = ("y", "zl", "c")
TENSOR = ("zh", "x")
CHIP = ("y", "zl")

low_score = -1e30


def shifted(block, axes, size, distance, wrap=False):
    if wrap:
        route = [(i, (i + distance) % size) for i in range(size)]
    else:
        route = [(i, i + distance) for i in range(size) if 0 <= i + distance < size]
    return lax.ppermute(block, axes, route)


def swap_cores(block):
    return lax.ppermute(block, "c", [(0, 1), (1, 0)])


def clip_index(positions, clip_ends):
    return jnp.sum((positions[:, None] >= clip_ends[None, :]).astype(jnp.int32), axis=1)


def allowed_keys(query_clip, source, clip_ends, page_table, page_count, block_total, row_count):
    key_pos = source * row_count + jnp.arange(row_count, dtype=jnp.int32)
    in_range = (source >= 0) & (source < block_total)
    same_clip = (query_clip[:, None] == clip_index(key_pos, clip_ends)[None, :]) & in_range
    clip_total = clip_ends.shape[0]
    page_ids = source * POOL + jnp.arange(POOL, dtype=jnp.int32)
    live_slots = jnp.arange(page_table.shape[1], dtype=jnp.int32)[None, :] < page_count[:, None]
    named_pages = jnp.any(
        live_slots[:, :, None] & (page_table[:, :, None] == page_ids[None, None, :]), axis=1
    )
    member = query_clip[:, None] == jnp.arange(clip_total, dtype=jnp.int32)[None, :]
    page_ok = jnp.any(member[:, :, None] & named_pages[None], axis=1) & in_range
    page_ok = jnp.repeat(page_ok, PAGE, axis=1)
    return jnp.concatenate([same_clip, page_ok], axis=1)


def attend(carry_state, query_heads, key_heads, value_heads, allowed):
    running_max, totals, accumulated = carry_state
    scores = jnp.einsum(
        "qhd,khd->hqk", query_heads, key_heads, preferred_element_type=jnp.float32
    ) * (1.0 / math.sqrt(HD))
    scores = jnp.where(allowed[None], scores, low_score)
    new_max = jnp.maximum(running_max, jnp.max(scores, axis=2))
    factor = jnp.exp(running_max - new_max)
    weights = jnp.where(allowed[None], jnp.exp(scores - new_max[:, :, None]), 0.0)
    totals = totals * factor + jnp.sum(weights, axis=2)
    accumulated = accumulated * factor[:, :, None] + jnp.einsum(
        "hqk,khd->hqd",
        weights.astype(jnp.bfloat16),
        value_heads,
        preferred_element_type=jnp.float32,
    )
    return (new_max, totals, accumulated)


def empty_state(head_count, row_count):
    return (
        jnp.full((head_count, row_count), low_score, jnp.float32),
        jnp.zeros((head_count, row_count), jnp.float32),
        jnp.zeros((head_count, row_count, HD), jnp.float32),
    )


def visit_block(carry_state, packed, source, query_heads, query_clip, context):
    clip_ends, page_table, page_count, block_total = context
    row_count = query_heads.shape[0]
    head_count = query_heads.shape[1]
    allowed = allowed_keys(
        query_clip, source, clip_ends, page_table, page_count, block_total, row_count
    )
    key_heads = packed[0].reshape(-1, head_count, HD)
    value_heads = packed[1].reshape(-1, head_count, HD)
    return attend(carry_state, query_heads, key_heads, value_heads, allowed)


def gather_weight(out_weight, sizes, is_first):
    n_y, n_zl = sizes["y"], sizes["zl"]
    rows, cols = out_weight.shape
    other = swap_cores(out_weight)
    pair = jnp.where(
        is_first,
        jnp.concatenate([out_weight, other], axis=0),
        jnp.concatenate([other, out_weight], axis=0),
    )
    zl = lax.axis_index("zl")
    row_block = jnp.zeros((n_zl, 2 * rows, cols), out_weight.dtype)
    row_block = lax.dynamic_update_index_in_dim(row_block, pair, zl, 0)
    for d in range(1, n_zl):
        got = shifted(pair, "zl", n_zl, d, wrap=True)
        row_block = lax.dynamic_update_index_in_dim(row_block, got, (zl - d) % n_zl, 0)
    return row_block.reshape(n_zl * 2 * rows, cols)


def spread_weight(row_block, sizes, is_first):
    n_y = sizes["y"]
    y = lax.axis_index("y")
    cols = row_block.shape[1]
    full = jnp.zeros((n_y,) + row_block.shape, row_block.dtype)
    full = lax.dynamic_update_index_in_dim(full, row_block, y, 0)
    below_count = n_y // 2
    above_count = (n_y - 1) // 2
    received = []
    for j in range(1, below_count + 1):
        route = [(yy * 2, ((yy + j) % n_y) * 2) for yy in range(n_y)]
        if j <= above_count:
            route += [(yy * 2 + 1, ((yy - j) % n_y) * 2 + 1) for yy in range(n_y)]
        received.append(lax.ppermute(row_block, ("y", "c"), route))
    traded = swap_cores(jnp.stack(received))
    for j in range(1, below_count + 1):
        got = received[j - 1]
        if j <= above_count:
            here = jnp.where(is_first, (y - j) % n_y, (y + j) % n_y)
            there = jnp.where(is_first, (y + j) % n_y, (y - j) % n_y)
            full = lax.dynamic_update_index_in_dim(full, got, here, 0)
            full = lax.dynamic_update_index_in_dim(full, traded[j - 1], there, 0)
        else:
            value = jnp.where(is_first, got, traded[j - 1])
            full = lax.dynamic_update_index_in_dim(full, value, (y - j) % n_y, 0)
    return full.reshape(n_y * row_block.shape[0], cols)


def gather_attention(attention_local, sizes):
    n_x = sizes["x"]
    n_tensor = sizes["zh"] * n_x
    row_count, width = attention_local.shape
    zh = lax.axis_index("zh")
    x = lax.axis_index("x")
    partner = lax.ppermute(attention_local, "zh", [(0, 1), (1, 0)])
    both = jnp.where(
        zh == 0,
        jnp.concatenate([attention_local, partner], axis=1),
        jnp.concatenate([partner, attention_local], axis=1),
    )
    pieces = [(both, x)]
    for d in range(1, n_x):
        pieces.append((shifted(both, "x", n_x, d, wrap=True), (x - d) % n_x))
    full = jnp.zeros((row_count, n_tensor * width), attention_local.dtype)
    for piece, piece_x in pieces:
        for half in range(2):
            start = pl_multiple((half * n_x + piece_x) * width)
            full = lax.dynamic_update_slice(
                full, piece[:, half * width:(half + 1) * width], (jnp.int32(0), start)
            )
    return full


def pl_multiple(value):
    return value.astype(jnp.int32)


def make_local(sizes):
    n_chip = sizes["y"] * sizes["zl"]

    def local(
        queries,
        key_tiles,
        value_tiles,
        cache_keys,
        cache_values,
        hidden,
        out_weight,
        gate_table,
        lengths,
        page_table,
        page_count,
        timestep,
    ):
        row_count = queries.shape[0]
        tile_width = queries.shape[1]
        head_count = tile_width // HD
        block_total = n_chip * 2
        chip = lax.axis_index("y") * sizes["zl"] + lax.axis_index("zl")
        core = lax.axis_index("c")
        is_first = core == 0
        seq_index = chip * 2 + core
        clip_ends = jnp.cumsum(lengths, dtype=jnp.int32)
        row_ids = jnp.arange(row_count, dtype=jnp.int32)
        positions = seq_index * row_count + row_ids
        query_clip = clip_index(positions, clip_ends)
        query_heads = queries.reshape(row_count, head_count, HD)
        context = (clip_ends, page_table, page_count, block_total)
        packed = jnp.stack(
            [
                jnp.concatenate([key_tiles, cache_keys.reshape(-1, tile_width)], axis=0),
                jnp.concatenate([value_tiles, cache_values.reshape(-1, tile_width)], axis=0),
            ]
        )
        row_block = gather_weight(out_weight, sizes, is_first)
        packed, row_block = lax.optimization_barrier((packed, row_block))
        weight_full = spread_weight(row_block, sizes, is_first)

        carry_state = visit_block(
            empty_state(head_count, row_count), packed, seq_index, query_heads, query_clip, context
        )
        above = {}
        below = {}
        for d in range(1, 4):
            above[d] = shifted(packed, CHIP, n_chip, -d)
            carry_state = visit_block(
                carry_state, above[d], seq_index + 2 * d, query_heads, query_clip, context
            )
            below[d] = shifted(packed, CHIP, n_chip, d)
            carry_state = visit_block(
                carry_state, below[d], seq_index - 2 * d, query_heads, query_clip, context
            )
        sign = 1 - 2 * core
        outgoing = [
            (packed, 1),
            (jnp.where(is_first, above[1], below[1]), -1),
            (jnp.where(is_first, above[2], below[2]), -3),
            (jnp.where(is_first, above[3], below[3]), -5),
            (jnp.where(is_first, below[1], above[1]), 3),
            (jnp.where(is_first, below[2], above[2]), 5),
        ]
        for block, offset in outgoing:
            got = swap_cores(block)
            carry_state = visit_block(
                carry_state, got, seq_index + sign * offset, query_heads, query_clip, context
            )
        running_max, totals, accumulated = carry_state
        result = accumulated / totals[:, :, None]
        attention_local = (
            jnp.transpose(result, (1, 0, 2)).reshape(row_count, tile_width).astype(jnp.bfloat16)
        )
        attention = gather_attention(attention_local, sizes)
        projected = jnp.dot(attention, weight_full, preferred_element_type=jnp.float32)
        clip_total = lengths.shape[0]
        step_onehot = (
            timestep[:, None] == jnp.arange(gate_table.shape[0], dtype=jnp.int32)[None, :]
        ).astype(jnp.float32)
        clip_gate = jnp.dot(
            step_onehot, gate_table, precision=lax.Precision.HIGHEST, preferred_element_type=jnp.float32
        )
        clip_onehot = (
            query_clip[:, None] == jnp.arange(clip_total, dtype=jnp.int32)[None, :]
        ).astype(jnp.float32)
        token_gate = jnp.dot(
            clip_onehot, clip_gate, precision=lax.Precision.HIGHEST, preferred_element_type=jnp.float32
        )
        return (hidden.astype(jnp.float32) + token_gate * projected).astype(jnp.bfloat16)

    return local


def solution(mesh):
    n_seq = mesh.shape["seq"]
    n_tensor = mesh.shape["tensor"]
    sizes = {"y": n_seq // 8, "zl": 4, "c": 2, "zh": 2, "x": n_tensor // 2}
    devices = np.asarray(mesh.devices).reshape(tuple(sizes[a] for a in AXES))
    fine = Mesh(devices, AXES)
    return jax.shard_map(
        make_local(sizes),
        mesh=fine,
        in_specs=(
            P(SEQ, TENSOR),
            P(SEQ, TENSOR),
            P(SEQ, TENSOR),
            P(SEQ, None, TENSOR),
            P(SEQ, None, TENSOR),
            P(SEQ, TENSOR),
            P(SEQ, TENSOR),
            P(None, TENSOR),
            P(),
            P(),
            P(),
            P(),
        ),
        out_specs=P(SEQ, TENSOR),
        check_vma=False,
    )
```

```python
import math

import numpy as np
import jax
import jax.numpy as jnp
from jax import lax
from jax.sharding import Mesh, PartitionSpec as P

HD = 128
PAGE = 128
POOL = 2
REACH = 6

AXES = ("y", "zl", "c", "zh", "x")
SEQ = ("y", "zl", "c")
TENSOR = ("zh", "x")
CHIP = ("y", "zl")

low_score = -1e30


def shifted(block, axes, size, distance, wrap=False):
    if wrap:
        route = [(i, (i + distance) % size) for i in range(size)]
    else:
        route = [(i, i + distance) for i in range(size) if 0 <= i + distance < size]
    return lax.ppermute(block, axes, route)


def swap_cores(block):
    return lax.ppermute(block, "c", [(0, 1), (1, 0)])


def clip_index(positions, clip_ends):
    return jnp.sum((positions[:, None] >= clip_ends[None, :]).astype(jnp.int32), axis=1)


def allowed_keys(query_clip, source, clip_ends, page_table, page_count, block_total, row_count):
    key_pos = source * row_count + jnp.arange(row_count, dtype=jnp.int32)
    in_range = (source >= 0) & (source < block_total)
    same_clip = (query_clip[:, None] == clip_index(key_pos, clip_ends)[None, :]) & in_range
    clip_total = clip_ends.shape[0]
    page_ids = source * POOL + jnp.arange(POOL, dtype=jnp.int32)
    live_slots = jnp.arange(page_table.shape[1], dtype=jnp.int32)[None, :] < page_count[:, None]
    named_pages = jnp.any(
        live_slots[:, :, None] & (page_table[:, :, None] == page_ids[None, None, :]), axis=1
    )
    member = query_clip[:, None] == jnp.arange(clip_total, dtype=jnp.int32)[None, :]
    page_ok = jnp.any(member[:, :, None] & named_pages[None], axis=1) & in_range
    page_ok = jnp.repeat(page_ok, PAGE, axis=1)
    return jnp.concatenate([same_clip, page_ok], axis=1)


def attend(carry_state, query_heads, key_heads, value_heads, allowed):
    running_max, totals, accumulated = carry_state
    scores = jnp.einsum(
        "qhd,khd->hqk", query_heads, key_heads, preferred_element_type=jnp.float32
    ) * (1.0 / math.sqrt(HD))
    scores = jnp.where(allowed[None], scores, low_score)
    new_max = jnp.maximum(running_max, jnp.max(scores, axis=2))
    factor = jnp.exp(running_max - new_max)
    weights = jnp.where(allowed[None], jnp.exp(scores - new_max[:, :, None]), 0.0)
    totals = totals * factor + jnp.sum(weights, axis=2)
    accumulated = accumulated * factor[:, :, None] + jnp.einsum(
        "hqk,khd->hqd",
        weights.astype(jnp.bfloat16),
        value_heads,
        preferred_element_type=jnp.float32,
    )
    return (new_max, totals, accumulated)


def empty_state(head_count, row_count):
    return (
        jnp.full((head_count, row_count), low_score, jnp.float32),
        jnp.zeros((head_count, row_count), jnp.float32),
        jnp.zeros((head_count, row_count, HD), jnp.float32),
    )


def visit_block(carry_state, packed, source, query_heads, query_clip, context):
    clip_ends, page_table, page_count, block_total = context
    row_count = query_heads.shape[0]
    head_count = query_heads.shape[1]
    allowed = allowed_keys(
        query_clip, source, clip_ends, page_table, page_count, block_total, row_count
    )
    key_heads = packed[0].reshape(-1, head_count, HD)
    value_heads = packed[1].reshape(-1, head_count, HD)
    return attend(carry_state, query_heads, key_heads, value_heads, allowed)


def gather_weight(out_weight, sizes, is_first):
    n_y, n_zl = sizes["y"], sizes["zl"]
    rows, cols = out_weight.shape
    other = swap_cores(out_weight)
    pair = jnp.where(
        is_first,
        jnp.concatenate([out_weight, other], axis=0),
        jnp.concatenate([other, out_weight], axis=0),
    )
    zl = lax.axis_index("zl")
    row_block = jnp.zeros((n_zl, 2 * rows, cols), out_weight.dtype)
    row_block = lax.dynamic_update_index_in_dim(row_block, pair, zl, 0)
    for d in range(1, n_zl):
        got = shifted(pair, "zl", n_zl, d, wrap=True)
        row_block = lax.dynamic_update_index_in_dim(row_block, got, (zl - d) % n_zl, 0)
    return row_block.reshape(n_zl * 2 * rows, cols)


def spread_weight(row_block, sizes, is_first):
    n_y = sizes["y"]
    y = lax.axis_index("y")
    cols = row_block.shape[1]
    full = jnp.zeros((n_y,) + row_block.shape, row_block.dtype)
    full = lax.dynamic_update_index_in_dim(full, row_block, y, 0)
    below_count = n_y // 2
    above_count = (n_y - 1) // 2
    received = []
    for j in range(1, below_count + 1):
        route = [(yy * 2, ((yy + j) % n_y) * 2) for yy in range(n_y)]
        if j <= above_count:
            route += [(yy * 2 + 1, ((yy - j) % n_y) * 2 + 1) for yy in range(n_y)]
        received.append(lax.ppermute(row_block, ("y", "c"), route))
    traded = swap_cores(jnp.stack(received))
    for j in range(1, below_count + 1):
        got = received[j - 1]
        if j <= above_count:
            here = jnp.where(is_first, (y - j) % n_y, (y + j) % n_y)
            there = jnp.where(is_first, (y + j) % n_y, (y - j) % n_y)
            full = lax.dynamic_update_index_in_dim(full, got, here, 0)
            full = lax.dynamic_update_index_in_dim(full, traded[j - 1], there, 0)
        else:
            value = jnp.where(is_first, got, traded[j - 1])
            full = lax.dynamic_update_index_in_dim(full, value, (y - j) % n_y, 0)
    return full.reshape(n_y * row_block.shape[0], cols)


def gather_attention(attention_local, sizes):
    n_x = sizes["x"]
    n_tensor = sizes["zh"] * n_x
    row_count, width = attention_local.shape
    zh = lax.axis_index("zh")
    x = lax.axis_index("x")
    partner = lax.ppermute(attention_local, "zh", [(0, 1), (1, 0)])
    both = jnp.where(
        zh == 0,
        jnp.concatenate([attention_local, partner], axis=1),
        jnp.concatenate([partner, attention_local], axis=1),
    )
    pieces = [(both, x)]
    for d in range(1, n_x):
        pieces.append((shifted(both, "x", n_x, d, wrap=True), (x - d) % n_x))
    full = jnp.zeros((row_count, n_tensor * width), attention_local.dtype)
    for piece, piece_x in pieces:
        for half in range(2):
            start = pl_multiple((half * n_x + piece_x) * width)
            full = lax.dynamic_update_slice(
                full, piece[:, half * width:(half + 1) * width], (jnp.int32(0), start)
            )
    return full


def pl_multiple(value):
    return value.astype(jnp.int32)


def make_local(sizes):
    n_chip = sizes["y"] * sizes["zl"]

    def local(
        queries,
        key_tiles,
        value_tiles,
        cache_keys,
        cache_values,
        hidden,
        out_weight,
        gate_table,
        lengths,
        page_table,
        page_count,
        timestep,
    ):
        row_count = queries.shape[0]
        tile_width = queries.shape[1]
        head_count = tile_width // HD
        block_total = n_chip * 2
        chip = lax.axis_index("y") * sizes["zl"] + lax.axis_index("zl")
        core = lax.axis_index("c")
        is_first = core == 0
        seq_index = chip * 2 + core
        clip_ends = jnp.cumsum(lengths, dtype=jnp.int32)
        row_ids = jnp.arange(row_count, dtype=jnp.int32)
        positions = seq_index * row_count + row_ids
        query_clip = clip_index(positions, clip_ends)
        query_heads = queries.reshape(row_count, head_count, HD)
        context = (clip_ends, page_table, page_count, block_total)
        packed = jnp.stack(
            [
                jnp.concatenate([key_tiles, cache_keys.reshape(-1, tile_width)], axis=0),
                jnp.concatenate([value_tiles, cache_values.reshape(-1, tile_width)], axis=0),
            ]
        )

        carry_state = visit_block(
            empty_state(head_count, row_count), packed, seq_index, query_heads, query_clip, context
        )
        above = {}
        below = {}
        for d in range(1, 4):
            above[d] = shifted(packed, CHIP, n_chip, -d)
            carry_state = visit_block(
                carry_state, above[d], seq_index + 2 * d, query_heads, query_clip, context
            )
            below[d] = shifted(packed, CHIP, n_chip, d)
            carry_state = visit_block(
                carry_state, below[d], seq_index - 2 * d, query_heads, query_clip, context
            )
        sign = 1 - 2 * core
        gated = lax.optimization_barrier(
            (out_weight, above[1], above[2], above[3], below[1], below[2], below[3])
        )
        out_weight = gated[0]
        above = dict(zip((1, 2, 3), gated[1:4]))
        below = dict(zip((1, 2, 3), gated[4:7]))
        weight_full = spread_weight(gather_weight(out_weight, sizes, is_first), sizes, is_first)
        outgoing = [
            (packed, 1),
            (jnp.where(is_first, above[1], below[1]), -1),
            (jnp.where(is_first, above[2], below[2]), -3),
            (jnp.where(is_first, above[3], below[3]), -5),
            (jnp.where(is_first, below[1], above[1]), 3),
            (jnp.where(is_first, below[2], above[2]), 5),
        ]
        for block, offset in outgoing:
            got = swap_cores(block)
            carry_state = visit_block(
                carry_state, got, seq_index + sign * offset, query_heads, query_clip, context
            )
        running_max, totals, accumulated = carry_state
        result = accumulated / totals[:, :, None]
        attention_local = (
            jnp.transpose(result, (1, 0, 2)).reshape(row_count, tile_width).astype(jnp.bfloat16)
        )
        attention = gather_attention(attention_local, sizes)
        projected = jnp.dot(attention, weight_full, preferred_element_type=jnp.float32)
        clip_total = lengths.shape[0]
        step_onehot = (
            timestep[:, None] == jnp.arange(gate_table.shape[0], dtype=jnp.int32)[None, :]
        ).astype(jnp.float32)
        clip_gate = jnp.dot(
            step_onehot, gate_table, precision=lax.Precision.HIGHEST, preferred_element_type=jnp.float32
        )
        clip_onehot = (
            query_clip[:, None] == jnp.arange(clip_total, dtype=jnp.int32)[None, :]
        ).astype(jnp.float32)
        token_gate = jnp.dot(
            clip_onehot, clip_gate, precision=lax.Precision.HIGHEST, preferred_element_type=jnp.float32
        )
        return (hidden.astype(jnp.float32) + token_gate * projected).astype(jnp.bfloat16)

    return local


def solution(mesh):
    n_seq = mesh.shape["seq"]
    n_tensor = mesh.shape["tensor"]
    sizes = {"y": n_seq // 8, "zl": 4, "c": 2, "zh": 2, "x": n_tensor // 2}
    devices = np.asarray(mesh.devices).reshape(tuple(sizes[a] for a in AXES))
    fine = Mesh(devices, AXES)
    return jax.shard_map(
        make_local(sizes),
        mesh=fine,
        in_specs=(
            P(SEQ, TENSOR),
            P(SEQ, TENSOR),
            P(SEQ, TENSOR),
            P(SEQ, None, TENSOR),
            P(SEQ, None, TENSOR),
            P(SEQ, TENSOR),
            P(SEQ, TENSOR),
            P(None, TENSOR),
            P(),
            P(),
            P(),
            P(),
        ),
        out_specs=P(SEQ, TENSOR),
        check_vma=False,
    )
```

```python
import math

import numpy as np
import jax
import jax.numpy as jnp
from jax import lax
from jax.sharding import Mesh, PartitionSpec as P

HD = 128
PAGE = 128
POOL = 2
REACH = 6

AXES = ("y", "zl", "c", "zh", "x")
SEQ = ("y", "zl", "c")
TENSOR = ("zh", "x")
CHIP = ("y", "zl")

low_score = -1e30


def shifted(block, axes, size, distance, wrap=False):
    if wrap:
        route = [(i, (i + distance) % size) for i in range(size)]
    else:
        route = [(i, i + distance) for i in range(size) if 0 <= i + distance < size]
    return lax.ppermute(block, axes, route)


def swap_cores(block):
    return lax.ppermute(block, "c", [(0, 1), (1, 0)])


def clip_index(positions, clip_ends):
    return jnp.sum((positions[:, None] >= clip_ends[None, :]).astype(jnp.int32), axis=1)


def allowed_keys(query_clip, source, clip_ends, page_table, page_count, block_total, row_count):
    key_pos = source * row_count + jnp.arange(row_count, dtype=jnp.int32)
    in_range = (source >= 0) & (source < block_total)
    same_clip = (query_clip[:, None] == clip_index(key_pos, clip_ends)[None, :]) & in_range
    clip_total = clip_ends.shape[0]
    page_ids = source * POOL + jnp.arange(POOL, dtype=jnp.int32)
    live_slots = jnp.arange(page_table.shape[1], dtype=jnp.int32)[None, :] < page_count[:, None]
    named_pages = jnp.any(
        live_slots[:, :, None] & (page_table[:, :, None] == page_ids[None, None, :]), axis=1
    )
    member = query_clip[:, None] == jnp.arange(clip_total, dtype=jnp.int32)[None, :]
    page_ok = jnp.any(member[:, :, None] & named_pages[None], axis=1) & in_range
    page_ok = jnp.repeat(page_ok, PAGE, axis=1)
    return jnp.concatenate([same_clip, page_ok], axis=1)


def attend(carry_state, query_heads, key_heads, value_heads, allowed):
    running_max, totals, accumulated = carry_state
    scores = jnp.einsum(
        "qhd,khd->hqk", query_heads, key_heads, preferred_element_type=jnp.float32
    ) * (1.0 / math.sqrt(HD))
    scores = jnp.where(allowed[None], scores, low_score)
    new_max = jnp.maximum(running_max, jnp.max(scores, axis=2))
    factor = jnp.exp(running_max - new_max)
    weights = jnp.where(allowed[None], jnp.exp(scores - new_max[:, :, None]), 0.0)
    totals = totals * factor + jnp.sum(weights, axis=2)
    accumulated = accumulated * factor[:, :, None] + jnp.einsum(
        "hqk,khd->hqd",
        weights.astype(jnp.bfloat16),
        value_heads,
        preferred_element_type=jnp.float32,
    )
    return (new_max, totals, accumulated)


def empty_state(head_count, row_count):
    return (
        jnp.full((head_count, row_count), low_score, jnp.float32),
        jnp.zeros((head_count, row_count), jnp.float32),
        jnp.zeros((head_count, row_count, HD), jnp.float32),
    )


def visit_block(carry_state, packed, source, query_heads, query_clip, context):
    clip_ends, page_table, page_count, block_total = context
    row_count = query_heads.shape[0]
    head_count = query_heads.shape[1]
    allowed = allowed_keys(
        query_clip, source, clip_ends, page_table, page_count, block_total, row_count
    )
    key_heads = packed[0].reshape(-1, head_count, HD)
    value_heads = packed[1].reshape(-1, head_count, HD)
    return attend(carry_state, query_heads, key_heads, value_heads, allowed)


def gather_weight(out_weight, sizes, is_first):
    n_y, n_zl = sizes["y"], sizes["zl"]
    rows, cols = out_weight.shape
    other = swap_cores(out_weight)
    pair = jnp.where(
        is_first,
        jnp.concatenate([out_weight, other], axis=0),
        jnp.concatenate([other, out_weight], axis=0),
    )
    zl = lax.axis_index("zl")
    row_block = jnp.zeros((n_zl, 2 * rows, cols), out_weight.dtype)
    row_block = lax.dynamic_update_index_in_dim(row_block, pair, zl, 0)
    for d in range(1, n_zl):
        got = shifted(pair, "zl", n_zl, d, wrap=True)
        row_block = lax.dynamic_update_index_in_dim(row_block, got, (zl - d) % n_zl, 0)
    return row_block.reshape(n_zl * 2 * rows, cols)


def spread_weight(row_block, sizes, is_first):
    n_y = sizes["y"]
    y = lax.axis_index("y")
    cols = row_block.shape[1]
    full = jnp.zeros((n_y,) + row_block.shape, row_block.dtype)
    full = lax.dynamic_update_index_in_dim(full, row_block, y, 0)
    below_count = n_y // 2
    above_count = (n_y - 1) // 2
    received = []
    for j in range(1, below_count + 1):
        route = [(yy * 2, ((yy + j) % n_y) * 2) for yy in range(n_y)]
        if j <= above_count:
            route += [(yy * 2 + 1, ((yy - j) % n_y) * 2 + 1) for yy in range(n_y)]
        received.append(lax.ppermute(row_block, ("y", "c"), route))
    traded = swap_cores(jnp.stack(received))
    for j in range(1, below_count + 1):
        got = received[j - 1]
        if j <= above_count:
            here = jnp.where(is_first, (y - j) % n_y, (y + j) % n_y)
            there = jnp.where(is_first, (y + j) % n_y, (y - j) % n_y)
            full = lax.dynamic_update_index_in_dim(full, got, here, 0)
            full = lax.dynamic_update_index_in_dim(full, traded[j - 1], there, 0)
        else:
            value = jnp.where(is_first, got, traded[j - 1])
            full = lax.dynamic_update_index_in_dim(full, value, (y - j) % n_y, 0)
    return full.reshape(n_y * row_block.shape[0], cols)


def gather_attention(attention_local, sizes):
    n_x = sizes["x"]
    n_tensor = sizes["zh"] * n_x
    row_count, width = attention_local.shape
    zh = lax.axis_index("zh")
    x = lax.axis_index("x")
    partner = lax.ppermute(attention_local, "zh", [(0, 1), (1, 0)])
    both = jnp.where(
        zh == 0,
        jnp.concatenate([attention_local, partner], axis=1),
        jnp.concatenate([partner, attention_local], axis=1),
    )
    pieces = [(both, x)]
    for d in range(1, n_x):
        pieces.append((shifted(both, "x", n_x, d, wrap=True), (x - d) % n_x))
    full = jnp.zeros((row_count, n_tensor * width), attention_local.dtype)
    for piece, piece_x in pieces:
        for half in range(2):
            start = pl_multiple((half * n_x + piece_x) * width)
            full = lax.dynamic_update_slice(
                full, piece[:, half * width:(half + 1) * width], (jnp.int32(0), start)
            )
    return full


def pl_multiple(value):
    return value.astype(jnp.int32)


def make_local(sizes):
    n_chip = sizes["y"] * sizes["zl"]

    def local(
        queries,
        key_tiles,
        value_tiles,
        cache_keys,
        cache_values,
        hidden,
        out_weight,
        gate_table,
        lengths,
        page_table,
        page_count,
        timestep,
    ):
        row_count = queries.shape[0]
        tile_width = queries.shape[1]
        head_count = tile_width // HD
        block_total = n_chip * 2
        chip = lax.axis_index("y") * sizes["zl"] + lax.axis_index("zl")
        core = lax.axis_index("c")
        is_first = core == 0
        seq_index = chip * 2 + core
        clip_ends = jnp.cumsum(lengths, dtype=jnp.int32)
        row_ids = jnp.arange(row_count, dtype=jnp.int32)
        positions = seq_index * row_count + row_ids
        query_clip = clip_index(positions, clip_ends)
        query_heads = queries.reshape(row_count, head_count, HD)
        context = (clip_ends, page_table, page_count, block_total)
        packed = jnp.stack(
            [
                jnp.concatenate([key_tiles, cache_keys.reshape(-1, tile_width)], axis=0),
                jnp.concatenate([value_tiles, cache_values.reshape(-1, tile_width)], axis=0),
            ]
        )
        weight_full = out_weight
        for axis in ("c", "zl", "y"):
            weight_full = lax.all_gather(weight_full, axis, axis=0, tiled=True)

        carry_state = visit_block(
            empty_state(head_count, row_count), packed, seq_index, query_heads, query_clip, context
        )
        above = {}
        below = {}
        for d in range(1, 4):
            above[d] = shifted(packed, CHIP, n_chip, -d)
            carry_state = visit_block(
                carry_state, above[d], seq_index + 2 * d, query_heads, query_clip, context
            )
            below[d] = shifted(packed, CHIP, n_chip, d)
            carry_state = visit_block(
                carry_state, below[d], seq_index - 2 * d, query_heads, query_clip, context
            )
        sign = 1 - 2 * core
        outgoing = [
            (packed, 1),
            (jnp.where(is_first, above[1], below[1]), -1),
            (jnp.where(is_first, above[2], below[2]), -3),
            (jnp.where(is_first, above[3], below[3]), -5),
            (jnp.where(is_first, below[1], above[1]), 3),
            (jnp.where(is_first, below[2], above[2]), 5),
        ]
        for block, offset in outgoing:
            got = swap_cores(block)
            carry_state = visit_block(
                carry_state, got, seq_index + sign * offset, query_heads, query_clip, context
            )
        running_max, totals, accumulated = carry_state
        result = accumulated / totals[:, :, None]
        attention_local = (
            jnp.transpose(result, (1, 0, 2)).reshape(row_count, tile_width).astype(jnp.bfloat16)
        )
        attention = gather_attention(attention_local, sizes)
        projected = jnp.dot(attention, weight_full, preferred_element_type=jnp.float32)
        clip_total = lengths.shape[0]
        step_onehot = (
            timestep[:, None] == jnp.arange(gate_table.shape[0], dtype=jnp.int32)[None, :]
        ).astype(jnp.float32)
        clip_gate = jnp.dot(
            step_onehot, gate_table, precision=lax.Precision.HIGHEST, preferred_element_type=jnp.float32
        )
        clip_onehot = (
            query_clip[:, None] == jnp.arange(clip_total, dtype=jnp.int32)[None, :]
        ).astype(jnp.float32)
        token_gate = jnp.dot(
            clip_onehot, clip_gate, precision=lax.Precision.HIGHEST, preferred_element_type=jnp.float32
        )
        return (hidden.astype(jnp.float32) + token_gate * projected).astype(jnp.bfloat16)

    return local


def solution(mesh):
    n_seq = mesh.shape["seq"]
    n_tensor = mesh.shape["tensor"]
    sizes = {"y": n_seq // 8, "zl": 4, "c": 2, "zh": 2, "x": n_tensor // 2}
    devices = np.asarray(mesh.devices).reshape(tuple(sizes[a] for a in AXES))
    fine = Mesh(devices, AXES)
    return jax.shard_map(
        make_local(sizes),
        mesh=fine,
        in_specs=(
            P(SEQ, TENSOR),
            P(SEQ, TENSOR),
            P(SEQ, TENSOR),
            P(SEQ, None, TENSOR),
            P(SEQ, None, TENSOR),
            P(SEQ, TENSOR),
            P(SEQ, TENSOR),
            P(None, TENSOR),
            P(),
            P(),
            P(),
            P(),
        ),
        out_specs=P(SEQ, TENSOR),
        check_vma=False,
    )
```

```python
import math

import numpy as np
import jax
import jax.numpy as jnp
from jax import lax
from jax.sharding import Mesh, PartitionSpec as P

HD = 128
PAGE = 128
POOL = 2
REACH = 6

AXES = ("y", "zl", "c", "zh", "x")
SEQ = ("y", "zl", "c")
TENSOR = ("zh", "x")
CHIP = ("y", "zl")

low_score = -1e30


def shifted(block, axes, size, distance, wrap=False):
    if wrap:
        route = [(i, (i + distance) % size) for i in range(size)]
    else:
        route = [(i, i + distance) for i in range(size) if 0 <= i + distance < size]
    return lax.ppermute(block, axes, route)


def swap_cores(block):
    return lax.ppermute(block, "c", [(0, 1), (1, 0)])


def clip_index(positions, clip_ends):
    return jnp.sum((positions[:, None] >= clip_ends[None, :]).astype(jnp.int32), axis=1)


def allowed_keys(query_clip, source, clip_ends, page_table, page_count, block_total, row_count):
    key_pos = source * row_count + jnp.arange(row_count, dtype=jnp.int32)
    in_range = (source >= 0) & (source < block_total)
    same_clip = (query_clip[:, None] == clip_index(key_pos, clip_ends)[None, :]) & in_range
    clip_total = clip_ends.shape[0]
    page_ids = source * POOL + jnp.arange(POOL, dtype=jnp.int32)
    live_slots = jnp.arange(page_table.shape[1], dtype=jnp.int32)[None, :] < page_count[:, None]
    named_pages = jnp.any(
        live_slots[:, :, None] & (page_table[:, :, None] == page_ids[None, None, :]), axis=1
    )
    member = query_clip[:, None] == jnp.arange(clip_total, dtype=jnp.int32)[None, :]
    page_ok = jnp.any(member[:, :, None] & named_pages[None], axis=1) & in_range
    page_ok = jnp.repeat(page_ok, PAGE, axis=1)
    return jnp.concatenate([same_clip, page_ok], axis=1)


def attend(carry_state, query_heads, key_heads, value_heads, allowed):
    running_max, totals, accumulated = carry_state
    scores = jnp.einsum(
        "qhd,khd->hqk", query_heads, key_heads, preferred_element_type=jnp.float32
    ) * (1.0 / math.sqrt(HD))
    scores = jnp.where(allowed[None], scores, low_score)
    new_max = jnp.maximum(running_max, jnp.max(scores, axis=2))
    factor = jnp.exp(running_max - new_max)
    weights = jnp.where(allowed[None], jnp.exp(scores - new_max[:, :, None]), 0.0)
    totals = totals * factor + jnp.sum(weights, axis=2)
    accumulated = accumulated * factor[:, :, None] + jnp.einsum(
        "hqk,khd->hqd",
        weights.astype(jnp.bfloat16),
        value_heads,
        preferred_element_type=jnp.float32,
    )
    return (new_max, totals, accumulated)


def empty_state(head_count, row_count):
    return (
        jnp.full((head_count, row_count), low_score, jnp.float32),
        jnp.zeros((head_count, row_count), jnp.float32),
        jnp.zeros((head_count, row_count, HD), jnp.float32),
    )


def visit_block(carry_state, packed, source, query_heads, query_clip, context):
    clip_ends, page_table, page_count, block_total = context
    row_count = query_heads.shape[0]
    head_count = query_heads.shape[1]
    allowed = allowed_keys(
        query_clip, source, clip_ends, page_table, page_count, block_total, row_count
    )
    key_heads = packed[0].reshape(-1, head_count, HD)
    value_heads = packed[1].reshape(-1, head_count, HD)
    return attend(carry_state, query_heads, key_heads, value_heads, allowed)


def gather_row_weight(out_weight, sizes):
    n_zl = sizes["zl"]
    zl = lax.axis_index("zl")
    row_part = jnp.zeros((n_zl,) + out_weight.shape, out_weight.dtype)
    row_part = lax.dynamic_update_index_in_dim(row_part, out_weight, zl, 0)
    for d in range(1, n_zl):
        got = shifted(out_weight, "zl", n_zl, d, wrap=True)
        row_part = lax.dynamic_update_index_in_dim(row_part, got, (zl - d) % n_zl, 0)
    return row_part


def gather_weight(out_weight, sizes, is_first):
    n_y, n_zl = sizes["y"], sizes["zl"]
    rows, cols = out_weight.shape
    other = swap_cores(out_weight)
    pair = jnp.where(
        is_first,
        jnp.concatenate([out_weight, other], axis=0),
        jnp.concatenate([other, out_weight], axis=0),
    )
    zl = lax.axis_index("zl")
    row_block = jnp.zeros((n_zl, 2 * rows, cols), out_weight.dtype)
    row_block = lax.dynamic_update_index_in_dim(row_block, pair, zl, 0)
    for d in range(1, n_zl):
        got = shifted(pair, "zl", n_zl, d, wrap=True)
        row_block = lax.dynamic_update_index_in_dim(row_block, got, (zl - d) % n_zl, 0)
    return row_block.reshape(n_zl * 2 * rows, cols)


def spread_weight(row_block, sizes, is_first):
    n_y = sizes["y"]
    y = lax.axis_index("y")
    cols = row_block.shape[1]
    full = jnp.zeros((n_y,) + row_block.shape, row_block.dtype)
    full = lax.dynamic_update_index_in_dim(full, row_block, y, 0)
    below_count = n_y // 2
    above_count = (n_y - 1) // 2
    received = []
    for j in range(1, below_count + 1):
        route = [(yy * 2, ((yy + j) % n_y) * 2) for yy in range(n_y)]
        if j <= above_count:
            route += [(yy * 2 + 1, ((yy - j) % n_y) * 2 + 1) for yy in range(n_y)]
        received.append(lax.ppermute(row_block, ("y", "c"), route))
    traded = swap_cores(jnp.stack(received))
    for j in range(1, below_count + 1):
        got = received[j - 1]
        if j <= above_count:
            here = jnp.where(is_first, (y - j) % n_y, (y + j) % n_y)
            there = jnp.where(is_first, (y + j) % n_y, (y - j) % n_y)
            full = lax.dynamic_update_index_in_dim(full, got, here, 0)
            full = lax.dynamic_update_index_in_dim(full, traded[j - 1], there, 0)
        else:
            value = jnp.where(is_first, got, traded[j - 1])
            full = lax.dynamic_update_index_in_dim(full, value, (y - j) % n_y, 0)
    return full.reshape(n_y * row_block.shape[0], cols)


def gather_attention(attention_local, sizes):
    n_x = sizes["x"]
    n_tensor = sizes["zh"] * n_x
    row_count, width = attention_local.shape
    zh = lax.axis_index("zh")
    x = lax.axis_index("x")
    partner = lax.ppermute(attention_local, "zh", [(0, 1), (1, 0)])
    both = jnp.where(
        zh == 0,
        jnp.concatenate([attention_local, partner], axis=1),
        jnp.concatenate([partner, attention_local], axis=1),
    )
    pieces = [(both, x)]
    for d in range(1, n_x):
        pieces.append((shifted(both, "x", n_x, d, wrap=True), (x - d) % n_x))
    full = jnp.zeros((row_count, n_tensor * width), attention_local.dtype)
    for piece, piece_x in pieces:
        for half in range(2):
            start = pl_multiple((half * n_x + piece_x) * width)
            full = lax.dynamic_update_slice(
                full, piece[:, half * width:(half + 1) * width], (jnp.int32(0), start)
            )
    return full


def pl_multiple(value):
    return value.astype(jnp.int32)


def make_local(sizes):
    n_chip = sizes["y"] * sizes["zl"]

    def local(
        queries,
        key_tiles,
        value_tiles,
        cache_keys,
        cache_values,
        hidden,
        out_weight,
        gate_table,
        lengths,
        page_table,
        page_count,
        timestep,
    ):
        row_count = queries.shape[0]
        tile_width = queries.shape[1]
        head_count = tile_width // HD
        block_total = n_chip * 2
        chip = lax.axis_index("y") * sizes["zl"] + lax.axis_index("zl")
        core = lax.axis_index("c")
        is_first = core == 0
        seq_index = chip * 2 + core
        clip_ends = jnp.cumsum(lengths, dtype=jnp.int32)
        row_ids = jnp.arange(row_count, dtype=jnp.int32)
        positions = seq_index * row_count + row_ids
        query_clip = clip_index(positions, clip_ends)
        query_heads = queries.reshape(row_count, head_count, HD)
        context = (clip_ends, page_table, page_count, block_total)
        packed = jnp.stack(
            [
                jnp.concatenate([key_tiles, cache_keys.reshape(-1, tile_width)], axis=0),
                jnp.concatenate([value_tiles, cache_values.reshape(-1, tile_width)], axis=0),
            ]
        )
        row_part = gather_row_weight(out_weight, sizes)
        packed, row_part = lax.optimization_barrier((packed, row_part))
        column = lax.all_gather(row_part, "y", axis=0)
        other = swap_cores(column)
        weight_full = jnp.where(
            is_first, jnp.stack([column, other], axis=2), jnp.stack([other, column], axis=2)
        ).reshape(-1, out_weight.shape[1])

        carry_state = visit_block(
            empty_state(head_count, row_count), packed, seq_index, query_heads, query_clip, context
        )
        above = {}
        below = {}
        for d in range(1, 4):
            above[d] = shifted(packed, CHIP, n_chip, -d)
            carry_state = visit_block(
                carry_state, above[d], seq_index + 2 * d, query_heads, query_clip, context
            )
            below[d] = shifted(packed, CHIP, n_chip, d)
            carry_state = visit_block(
                carry_state, below[d], seq_index - 2 * d, query_heads, query_clip, context
            )
        sign = 1 - 2 * core
        outgoing = [
            (packed, 1),
            (jnp.where(is_first, above[1], below[1]), -1),
            (jnp.where(is_first, above[2], below[2]), -3),
            (jnp.where(is_first, above[3], below[3]), -5),
            (jnp.where(is_first, below[1], above[1]), 3),
            (jnp.where(is_first, below[2], above[2]), 5),
        ]
        for block, offset in outgoing:
            got = swap_cores(block)
            carry_state = visit_block(
                carry_state, got, seq_index + sign * offset, query_heads, query_clip, context
            )
        running_max, totals, accumulated = carry_state
        result = accumulated / totals[:, :, None]
        attention_local = (
            jnp.transpose(result, (1, 0, 2)).reshape(row_count, tile_width).astype(jnp.bfloat16)
        )
        attention = gather_attention(attention_local, sizes)
        projected = jnp.dot(attention, weight_full, preferred_element_type=jnp.float32)
        clip_total = lengths.shape[0]
        step_onehot = (
            timestep[:, None] == jnp.arange(gate_table.shape[0], dtype=jnp.int32)[None, :]
        ).astype(jnp.float32)
        clip_gate = jnp.dot(
            step_onehot, gate_table, precision=lax.Precision.HIGHEST, preferred_element_type=jnp.float32
        )
        clip_onehot = (
            query_clip[:, None] == jnp.arange(clip_total, dtype=jnp.int32)[None, :]
        ).astype(jnp.float32)
        token_gate = jnp.dot(
            clip_onehot, clip_gate, precision=lax.Precision.HIGHEST, preferred_element_type=jnp.float32
        )
        return (hidden.astype(jnp.float32) + token_gate * projected).astype(jnp.bfloat16)

    return local


def solution(mesh):
    n_seq = mesh.shape["seq"]
    n_tensor = mesh.shape["tensor"]
    sizes = {"y": n_seq // 8, "zl": 4, "c": 2, "zh": 2, "x": n_tensor // 2}
    devices = np.asarray(mesh.devices).reshape(tuple(sizes[a] for a in AXES))
    fine = Mesh(devices, AXES)
    return jax.shard_map(
        make_local(sizes),
        mesh=fine,
        in_specs=(
            P(SEQ, TENSOR),
            P(SEQ, TENSOR),
            P(SEQ, TENSOR),
            P(SEQ, None, TENSOR),
            P(SEQ, None, TENSOR),
            P(SEQ, TENSOR),
            P(SEQ, TENSOR),
            P(None, TENSOR),
            P(),
            P(),
            P(),
            P(),
        ),
        out_specs=P(SEQ, TENSOR),
        check_vma=False,
    )
```

```python
import math

import numpy as np
import jax
import jax.numpy as jnp
from jax import lax
from jax.sharding import Mesh, PartitionSpec as P

HD = 128
PAGE = 128
POOL = 2
REACH = 6

AXES = ("y", "zl", "c", "zh", "x")
SEQ = ("y", "zl", "c")
TENSOR = ("zh", "x")
CHIP = ("y", "zl")

low_score = -1e30


def shifted(block, axes, size, distance, wrap=False):
    if wrap:
        route = [(i, (i + distance) % size) for i in range(size)]
    else:
        route = [(i, i + distance) for i in range(size) if 0 <= i + distance < size]
    return lax.ppermute(block, axes, route)


def swap_cores(block):
    return lax.ppermute(block, "c", [(0, 1), (1, 0)])


def clip_index(positions, clip_ends):
    return jnp.sum((positions[:, None] >= clip_ends[None, :]).astype(jnp.int32), axis=1)


def allowed_keys(query_clip, source, clip_ends, page_table, page_count, block_total, row_count):
    key_pos = source * row_count + jnp.arange(row_count, dtype=jnp.int32)
    in_range = (source >= 0) & (source < block_total)
    same_clip = (query_clip[:, None] == clip_index(key_pos, clip_ends)[None, :]) & in_range
    clip_total = clip_ends.shape[0]
    page_ids = source * POOL + jnp.arange(POOL, dtype=jnp.int32)
    live_slots = jnp.arange(page_table.shape[1], dtype=jnp.int32)[None, :] < page_count[:, None]
    named_pages = jnp.any(
        live_slots[:, :, None] & (page_table[:, :, None] == page_ids[None, None, :]), axis=1
    )
    member = query_clip[:, None] == jnp.arange(clip_total, dtype=jnp.int32)[None, :]
    page_ok = jnp.any(member[:, :, None] & named_pages[None], axis=1) & in_range
    page_ok = jnp.repeat(page_ok, PAGE, axis=1)
    return jnp.concatenate([same_clip, page_ok], axis=1)


def attend(carry_state, query_heads, key_heads, value_heads, allowed):
    running_max, totals, accumulated = carry_state
    scores = jnp.einsum(
        "qhd,khd->hqk", query_heads, key_heads, preferred_element_type=jnp.float32
    ) * (1.0 / math.sqrt(HD))
    scores = jnp.where(allowed[None], scores, low_score)
    new_max = jnp.maximum(running_max, jnp.max(scores, axis=2))
    factor = jnp.exp(running_max - new_max)
    weights = jnp.where(allowed[None], jnp.exp(scores - new_max[:, :, None]), 0.0)
    totals = totals * factor + jnp.sum(weights, axis=2)
    accumulated = accumulated * factor[:, :, None] + jnp.einsum(
        "hqk,khd->hqd",
        weights.astype(jnp.bfloat16),
        value_heads,
        preferred_element_type=jnp.float32,
    )
    return (new_max, totals, accumulated)


def empty_state(head_count, row_count):
    return (
        jnp.full((head_count, row_count), low_score, jnp.float32),
        jnp.zeros((head_count, row_count), jnp.float32),
        jnp.zeros((head_count, row_count, HD), jnp.float32),
    )


def visit_block(carry_state, packed, source, query_heads, query_clip, context):
    clip_ends, page_table, page_count, block_total = context
    row_count = query_heads.shape[0]
    head_count = query_heads.shape[1]
    allowed = allowed_keys(
        query_clip, source, clip_ends, page_table, page_count, block_total, row_count
    )
    key_heads = packed[0].reshape(-1, head_count, HD)
    value_heads = packed[1].reshape(-1, head_count, HD)
    return attend(carry_state, query_heads, key_heads, value_heads, allowed)


def gather_row_weight(out_weight, sizes):
    n_zl = sizes["zl"]
    zl = lax.axis_index("zl")
    row_part = jnp.zeros((n_zl,) + out_weight.shape, out_weight.dtype)
    row_part = lax.dynamic_update_index_in_dim(row_part, out_weight, zl, 0)
    for d in range(1, n_zl):
        got = shifted(out_weight, "zl", n_zl, d, wrap=True)
        row_part = lax.dynamic_update_index_in_dim(row_part, got, (zl - d) % n_zl, 0)
    return row_part


def gather_weight(out_weight, sizes, is_first):
    n_y, n_zl = sizes["y"], sizes["zl"]
    rows, cols = out_weight.shape
    other = swap_cores(out_weight)
    pair = jnp.where(
        is_first,
        jnp.concatenate([out_weight, other], axis=0),
        jnp.concatenate([other, out_weight], axis=0),
    )
    zl = lax.axis_index("zl")
    row_block = jnp.zeros((n_zl, 2 * rows, cols), out_weight.dtype)
    row_block = lax.dynamic_update_index_in_dim(row_block, pair, zl, 0)
    for d in range(1, n_zl):
        got = shifted(pair, "zl", n_zl, d, wrap=True)
        row_block = lax.dynamic_update_index_in_dim(row_block, got, (zl - d) % n_zl, 0)
    return row_block.reshape(n_zl * 2 * rows, cols)


def spread_weight(row_block, sizes, is_first):
    n_y = sizes["y"]
    y = lax.axis_index("y")
    cols = row_block.shape[1]
    full = jnp.zeros((n_y,) + row_block.shape, row_block.dtype)
    full = lax.dynamic_update_index_in_dim(full, row_block, y, 0)
    below_count = n_y // 2
    above_count = (n_y - 1) // 2
    received = []
    for j in range(1, below_count + 1):
        route = [(yy * 2, ((yy + j) % n_y) * 2) for yy in range(n_y)]
        if j <= above_count:
            route += [(yy * 2 + 1, ((yy - j) % n_y) * 2 + 1) for yy in range(n_y)]
        received.append(lax.ppermute(row_block, ("y", "c"), route))
    traded = swap_cores(jnp.stack(received))
    for j in range(1, below_count + 1):
        got = received[j - 1]
        if j <= above_count:
            here = jnp.where(is_first, (y - j) % n_y, (y + j) % n_y)
            there = jnp.where(is_first, (y + j) % n_y, (y - j) % n_y)
            full = lax.dynamic_update_index_in_dim(full, got, here, 0)
            full = lax.dynamic_update_index_in_dim(full, traded[j - 1], there, 0)
        else:
            value = jnp.where(is_first, got, traded[j - 1])
            full = lax.dynamic_update_index_in_dim(full, value, (y - j) % n_y, 0)
    return full.reshape(n_y * row_block.shape[0], cols)


def gather_attention(attention_local, sizes):
    n_x = sizes["x"]
    n_tensor = sizes["zh"] * n_x
    row_count, width = attention_local.shape
    zh = lax.axis_index("zh")
    x = lax.axis_index("x")
    partner = lax.ppermute(attention_local, "zh", [(0, 1), (1, 0)])
    both = jnp.where(
        zh == 0,
        jnp.concatenate([attention_local, partner], axis=1),
        jnp.concatenate([partner, attention_local], axis=1),
    )
    pieces = [(both, x)]
    for d in range(1, n_x):
        pieces.append((shifted(both, "x", n_x, d, wrap=True), (x - d) % n_x))
    full = jnp.zeros((row_count, n_tensor * width), attention_local.dtype)
    for piece, piece_x in pieces:
        for half in range(2):
            start = pl_multiple((half * n_x + piece_x) * width)
            full = lax.dynamic_update_slice(
                full, piece[:, half * width:(half + 1) * width], (jnp.int32(0), start)
            )
    return full


def pl_multiple(value):
    return value.astype(jnp.int32)


def make_local(sizes):
    n_chip = sizes["y"] * sizes["zl"]

    def local(
        queries,
        key_tiles,
        value_tiles,
        cache_keys,
        cache_values,
        hidden,
        out_weight,
        gate_table,
        lengths,
        page_table,
        page_count,
        timestep,
    ):
        row_count = queries.shape[0]
        tile_width = queries.shape[1]
        head_count = tile_width // HD
        block_total = n_chip * 2
        chip = lax.axis_index("y") * sizes["zl"] + lax.axis_index("zl")
        core = lax.axis_index("c")
        is_first = core == 0
        seq_index = chip * 2 + core
        clip_ends = jnp.cumsum(lengths, dtype=jnp.int32)
        row_ids = jnp.arange(row_count, dtype=jnp.int32)
        positions = seq_index * row_count + row_ids
        query_clip = clip_index(positions, clip_ends)
        query_heads = queries.reshape(row_count, head_count, HD)
        context = (clip_ends, page_table, page_count, block_total)
        packed = jnp.stack(
            [
                jnp.concatenate([key_tiles, cache_keys.reshape(-1, tile_width)], axis=0),
                jnp.concatenate([value_tiles, cache_values.reshape(-1, tile_width)], axis=0),
            ]
        )
        column = lax.all_gather(out_weight, CHIP, axis=0)
        other = swap_cores(column)
        weight_full = jnp.where(
            is_first, jnp.stack([column, other], axis=1), jnp.stack([other, column], axis=1)
        ).reshape(-1, out_weight.shape[1])

        carry_state = visit_block(
            empty_state(head_count, row_count), packed, seq_index, query_heads, query_clip, context
        )
        above = {}
        below = {}
        for d in range(1, 4):
            above[d] = shifted(packed, CHIP, n_chip, -d)
            carry_state = visit_block(
                carry_state, above[d], seq_index + 2 * d, query_heads, query_clip, context
            )
            below[d] = shifted(packed, CHIP, n_chip, d)
            carry_state = visit_block(
                carry_state, below[d], seq_index - 2 * d, query_heads, query_clip, context
            )
        sign = 1 - 2 * core
        outgoing = [
            (packed, 1),
            (jnp.where(is_first, above[1], below[1]), -1),
            (jnp.where(is_first, above[2], below[2]), -3),
            (jnp.where(is_first, above[3], below[3]), -5),
            (jnp.where(is_first, below[1], above[1]), 3),
            (jnp.where(is_first, below[2], above[2]), 5),
        ]
        for block, offset in outgoing:
            got = swap_cores(block)
            carry_state = visit_block(
                carry_state, got, seq_index + sign * offset, query_heads, query_clip, context
            )
        running_max, totals, accumulated = carry_state
        result = accumulated / totals[:, :, None]
        attention_local = (
            jnp.transpose(result, (1, 0, 2)).reshape(row_count, tile_width).astype(jnp.bfloat16)
        )
        attention = gather_attention(attention_local, sizes)
        projected = jnp.dot(attention, weight_full, preferred_element_type=jnp.float32)
        clip_total = lengths.shape[0]
        step_onehot = (
            timestep[:, None] == jnp.arange(gate_table.shape[0], dtype=jnp.int32)[None, :]
        ).astype(jnp.float32)
        clip_gate = jnp.dot(
            step_onehot, gate_table, precision=lax.Precision.HIGHEST, preferred_element_type=jnp.float32
        )
        clip_onehot = (
            query_clip[:, None] == jnp.arange(clip_total, dtype=jnp.int32)[None, :]
        ).astype(jnp.float32)
        token_gate = jnp.dot(
            clip_onehot, clip_gate, precision=lax.Precision.HIGHEST, preferred_element_type=jnp.float32
        )
        return (hidden.astype(jnp.float32) + token_gate * projected).astype(jnp.bfloat16)

    return local


def solution(mesh):
    n_seq = mesh.shape["seq"]
    n_tensor = mesh.shape["tensor"]
    sizes = {"y": n_seq // 8, "zl": 4, "c": 2, "zh": 2, "x": n_tensor // 2}
    devices = np.asarray(mesh.devices).reshape(tuple(sizes[a] for a in AXES))
    fine = Mesh(devices, AXES)
    return jax.shard_map(
        make_local(sizes),
        mesh=fine,
        in_specs=(
            P(SEQ, TENSOR),
            P(SEQ, TENSOR),
            P(SEQ, TENSOR),
            P(SEQ, None, TENSOR),
            P(SEQ, None, TENSOR),
            P(SEQ, TENSOR),
            P(SEQ, TENSOR),
            P(None, TENSOR),
            P(),
            P(),
            P(),
            P(),
        ),
        out_specs=P(SEQ, TENSOR),
        check_vma=False,
    )
```

```python
import math

import numpy as np
import jax
import jax.numpy as jnp
from jax import lax
from jax.sharding import Mesh, PartitionSpec as P

HD = 128
PAGE = 128
POOL = 2
REACH = 6

AXES = ("y", "zl", "c", "zh", "x")
SEQ = ("y", "zl", "c")
TENSOR = ("zh", "x")
CHIP = ("y", "zl")

low_score = -1e30


def shifted(block, axes, size, distance, wrap=False):
    if wrap:
        route = [(i, (i + distance) % size) for i in range(size)]
    else:
        route = [(i, i + distance) for i in range(size) if 0 <= i + distance < size]
    return lax.ppermute(block, axes, route)


def swap_cores(block):
    return lax.ppermute(block, "c", [(0, 1), (1, 0)])


def clip_index(positions, clip_ends):
    return jnp.sum((positions[:, None] >= clip_ends[None, :]).astype(jnp.int32), axis=1)


def allowed_keys(query_clip, source, clip_ends, page_table, page_count, block_total, row_count):
    key_pos = source * row_count + jnp.arange(row_count, dtype=jnp.int32)
    in_range = (source >= 0) & (source < block_total)
    same_clip = (query_clip[:, None] == clip_index(key_pos, clip_ends)[None, :]) & in_range
    clip_total = clip_ends.shape[0]
    page_ids = source * POOL + jnp.arange(POOL, dtype=jnp.int32)
    live_slots = jnp.arange(page_table.shape[1], dtype=jnp.int32)[None, :] < page_count[:, None]
    named_pages = jnp.any(
        live_slots[:, :, None] & (page_table[:, :, None] == page_ids[None, None, :]), axis=1
    )
    member = query_clip[:, None] == jnp.arange(clip_total, dtype=jnp.int32)[None, :]
    page_ok = jnp.any(member[:, :, None] & named_pages[None], axis=1) & in_range
    page_ok = jnp.repeat(page_ok, PAGE, axis=1)
    return jnp.concatenate([same_clip, page_ok], axis=1)


def attend(carry_state, query_heads, key_heads, value_heads, allowed):
    running_max, totals, accumulated = carry_state
    scores = jnp.einsum(
        "qhd,khd->hqk", query_heads, key_heads, preferred_element_type=jnp.float32
    ) * (1.0 / math.sqrt(HD))
    scores = jnp.where(allowed[None], scores, low_score)
    new_max = jnp.maximum(running_max, jnp.max(scores, axis=2))
    factor = jnp.exp(running_max - new_max)
    weights = jnp.where(allowed[None], jnp.exp(scores - new_max[:, :, None]), 0.0)
    totals = totals * factor + jnp.sum(weights, axis=2)
    accumulated = accumulated * factor[:, :, None] + jnp.einsum(
        "hqk,khd->hqd",
        weights.astype(jnp.bfloat16),
        value_heads,
        preferred_element_type=jnp.float32,
    )
    return (new_max, totals, accumulated)


def empty_state(head_count, row_count):
    return (
        jnp.full((head_count, row_count), low_score, jnp.float32),
        jnp.zeros((head_count, row_count), jnp.float32),
        jnp.zeros((head_count, row_count, HD), jnp.float32),
    )


def visit_block(carry_state, packed, source, query_heads, query_clip, context):
    clip_ends, page_table, page_count, block_total = context
    row_count = query_heads.shape[0]
    head_count = query_heads.shape[1]
    allowed = allowed_keys(
        query_clip, source, clip_ends, page_table, page_count, block_total, row_count
    )
    key_heads = packed[0].reshape(-1, head_count, HD)
    value_heads = packed[1].reshape(-1, head_count, HD)
    return attend(carry_state, query_heads, key_heads, value_heads, allowed)


def gather_weight(out_weight, sizes, is_first):
    n_y, n_zl = sizes["y"], sizes["zl"]
    rows, cols = out_weight.shape
    other = swap_cores(out_weight)
    pair = jnp.where(
        is_first,
        jnp.concatenate([out_weight, other], axis=0),
        jnp.concatenate([other, out_weight], axis=0),
    )
    zl = lax.axis_index("zl")
    row_block = jnp.zeros((n_zl, 2 * rows, cols), out_weight.dtype)
    row_block = lax.dynamic_update_index_in_dim(row_block, pair, zl, 0)
    for d in range(1, n_zl):
        got = shifted(pair, "zl", n_zl, d, wrap=True)
        row_block = lax.dynamic_update_index_in_dim(row_block, got, (zl - d) % n_zl, 0)
    return row_block.reshape(n_zl * 2 * rows, cols)


def spread_weight(row_block, sizes, is_first):
    n_y = sizes["y"]
    y = lax.axis_index("y")
    cols = row_block.shape[1]
    full = jnp.zeros((n_y,) + row_block.shape, row_block.dtype)
    full = lax.dynamic_update_index_in_dim(full, row_block, y, 0)
    below_count = n_y // 2
    above_count = (n_y - 1) // 2
    received = []
    for j in range(1, below_count + 1):
        route = [(yy * 2, ((yy + j) % n_y) * 2) for yy in range(n_y)]
        if j <= above_count:
            route += [(yy * 2 + 1, ((yy - j) % n_y) * 2 + 1) for yy in range(n_y)]
        received.append(lax.ppermute(row_block, ("y", "c"), route))
    traded = swap_cores(jnp.stack(received))
    for j in range(1, below_count + 1):
        got = received[j - 1]
        if j <= above_count:
            here = jnp.where(is_first, (y - j) % n_y, (y + j) % n_y)
            there = jnp.where(is_first, (y + j) % n_y, (y - j) % n_y)
            full = lax.dynamic_update_index_in_dim(full, got, here, 0)
            full = lax.dynamic_update_index_in_dim(full, traded[j - 1], there, 0)
        else:
            value = jnp.where(is_first, got, traded[j - 1])
            full = lax.dynamic_update_index_in_dim(full, value, (y - j) % n_y, 0)
    return full.reshape(n_y * row_block.shape[0], cols)


def gather_attention(attention_local, sizes):
    n_x = sizes["x"]
    n_tensor = sizes["zh"] * n_x
    row_count, width = attention_local.shape
    zh = lax.axis_index("zh")
    x = lax.axis_index("x")
    partner = lax.ppermute(attention_local, "zh", [(0, 1), (1, 0)])
    both = jnp.where(
        zh == 0,
        jnp.concatenate([attention_local, partner], axis=1),
        jnp.concatenate([partner, attention_local], axis=1),
    )
    pieces = [(both, x)]
    for d in range(1, n_x):
        pieces.append((shifted(both, "x", n_x, d, wrap=True), (x - d) % n_x))
    full = jnp.zeros((row_count, n_tensor * width), attention_local.dtype)
    for piece, piece_x in pieces:
        for half in range(2):
            start = pl_multiple((half * n_x + piece_x) * width)
            full = lax.dynamic_update_slice(
                full, piece[:, half * width:(half + 1) * width], (jnp.int32(0), start)
            )
    return full


def pl_multiple(value):
    return value.astype(jnp.int32)


def make_local(sizes):
    n_chip = sizes["y"] * sizes["zl"]

    def local(
        queries,
        key_tiles,
        value_tiles,
        cache_keys,
        cache_values,
        hidden,
        out_weight,
        gate_table,
        lengths,
        page_table,
        page_count,
        timestep,
    ):
        row_count = queries.shape[0]
        tile_width = queries.shape[1]
        head_count = tile_width // HD
        block_total = n_chip * 2
        chip = lax.axis_index("y") * sizes["zl"] + lax.axis_index("zl")
        core = lax.axis_index("c")
        is_first = core == 0
        seq_index = chip * 2 + core
        clip_ends = jnp.cumsum(lengths, dtype=jnp.int32)
        row_ids = jnp.arange(row_count, dtype=jnp.int32)
        positions = seq_index * row_count + row_ids
        query_clip = clip_index(positions, clip_ends)
        query_heads = queries.reshape(row_count, head_count, HD)
        context = (clip_ends, page_table, page_count, block_total)
        packed = jnp.stack(
            [
                jnp.concatenate([key_tiles, cache_keys.reshape(-1, tile_width)], axis=0),
                jnp.concatenate([value_tiles, cache_values.reshape(-1, tile_width)], axis=0),
            ]
        )
        row_block = gather_weight(out_weight, sizes, is_first)
        packed, row_block = lax.optimization_barrier((packed, row_block))
        weight_full = spread_weight(row_block, sizes, is_first)

        carry_state = visit_block(
            empty_state(head_count, row_count), packed, seq_index, query_heads, query_clip, context
        )
        above = {}
        below = {}
        for d in range(1, 4):
            above[d] = shifted(packed, CHIP, n_chip, -d)
            carry_state = visit_block(
                carry_state, above[d], seq_index + 2 * d, query_heads, query_clip, context
            )
            below[d] = shifted(packed, CHIP, n_chip, d)
            carry_state = visit_block(
                carry_state, below[d], seq_index - 2 * d, query_heads, query_clip, context
            )
        sign = 1 - 2 * core
        got = swap_cores(packed)
        carry_state = visit_block(
            carry_state, got, seq_index + sign, query_heads, query_clip, context
        )
        selected = jnp.where(
            is_first,
            jnp.stack([above[1], above[2], above[3], below[1], below[2]]),
            jnp.stack([below[1], below[2], below[3], above[1], above[2]]),
        )
        traded = swap_cores(selected)
        for slot, offset in enumerate((-1, -3, -5, 3, 5)):
            carry_state = visit_block(
                carry_state, traded[slot], seq_index + sign * offset, query_heads, query_clip, context
            )
        running_max, totals, accumulated = carry_state
        result = accumulated / totals[:, :, None]
        attention_local = (
            jnp.transpose(result, (1, 0, 2)).reshape(row_count, tile_width).astype(jnp.bfloat16)
        )
        attention = gather_attention(attention_local, sizes)
        projected = jnp.dot(attention, weight_full, preferred_element_type=jnp.float32)
        clip_total = lengths.shape[0]
        step_onehot = (
            timestep[:, None] == jnp.arange(gate_table.shape[0], dtype=jnp.int32)[None, :]
        ).astype(jnp.float32)
        clip_gate = jnp.dot(
            step_onehot, gate_table, precision=lax.Precision.HIGHEST, preferred_element_type=jnp.float32
        )
        clip_onehot = (
            query_clip[:, None] == jnp.arange(clip_total, dtype=jnp.int32)[None, :]
        ).astype(jnp.float32)
        token_gate = jnp.dot(
            clip_onehot, clip_gate, precision=lax.Precision.HIGHEST, preferred_element_type=jnp.float32
        )
        return (hidden.astype(jnp.float32) + token_gate * projected).astype(jnp.bfloat16)

    return local


def solution(mesh):
    n_seq = mesh.shape["seq"]
    n_tensor = mesh.shape["tensor"]
    sizes = {"y": n_seq // 8, "zl": 4, "c": 2, "zh": 2, "x": n_tensor // 2}
    devices = np.asarray(mesh.devices).reshape(tuple(sizes[a] for a in AXES))
    fine = Mesh(devices, AXES)
    return jax.shard_map(
        make_local(sizes),
        mesh=fine,
        in_specs=(
            P(SEQ, TENSOR),
            P(SEQ, TENSOR),
            P(SEQ, TENSOR),
            P(SEQ, None, TENSOR),
            P(SEQ, None, TENSOR),
            P(SEQ, TENSOR),
            P(SEQ, TENSOR),
            P(None, TENSOR),
            P(),
            P(),
            P(),
            P(),
        ),
        out_specs=P(SEQ, TENSOR),
        check_vma=False,
    )
```

```python
import math

import numpy as np
import jax
import jax.numpy as jnp
from jax import lax
from jax.sharding import Mesh, PartitionSpec as P

HD = 128
PAGE = 128
POOL = 2
REACH = 6

AXES = ("y", "zl", "c", "zh", "x")
SEQ = ("y", "zl", "c")
TENSOR = ("zh", "x")
CHIP = ("y", "zl")

low_score = -1e30


def shifted(block, axes, size, distance, wrap=False):
    if wrap:
        route = [(i, (i + distance) % size) for i in range(size)]
    else:
        route = [(i, i + distance) for i in range(size) if 0 <= i + distance < size]
    return lax.ppermute(block, axes, route)


def swap_cores(block):
    return lax.ppermute(block, "c", [(0, 1), (1, 0)])


def clip_index(positions, clip_ends):
    return jnp.sum((positions[:, None] >= clip_ends[None, :]).astype(jnp.int32), axis=1)


def allowed_keys(query_clip, source, clip_ends, page_table, page_count, block_total, row_count):
    key_pos = source * row_count + jnp.arange(row_count, dtype=jnp.int32)
    in_range = (source >= 0) & (source < block_total)
    same_clip = (query_clip[:, None] == clip_index(key_pos, clip_ends)[None, :]) & in_range
    clip_total = clip_ends.shape[0]
    page_ids = source * POOL + jnp.arange(POOL, dtype=jnp.int32)
    live_slots = jnp.arange(page_table.shape[1], dtype=jnp.int32)[None, :] < page_count[:, None]
    named_pages = jnp.any(
        live_slots[:, :, None] & (page_table[:, :, None] == page_ids[None, None, :]), axis=1
    )
    member = query_clip[:, None] == jnp.arange(clip_total, dtype=jnp.int32)[None, :]
    page_ok = jnp.any(member[:, :, None] & named_pages[None], axis=1) & in_range
    page_ok = jnp.repeat(page_ok, PAGE, axis=1)
    return jnp.concatenate([same_clip, page_ok], axis=1)


def attend(carry_state, query_heads, key_heads, value_heads, allowed):
    running_max, totals, accumulated = carry_state
    scores = jnp.einsum(
        "qhd,khd->hqk", query_heads, key_heads, preferred_element_type=jnp.float32
    ) * (1.0 / math.sqrt(HD))
    scores = jnp.where(allowed[None], scores, low_score)
    new_max = jnp.maximum(running_max, jnp.max(scores, axis=2))
    factor = jnp.exp(running_max - new_max)
    weights = jnp.where(allowed[None], jnp.exp(scores - new_max[:, :, None]), 0.0)
    totals = totals * factor + jnp.sum(weights, axis=2)
    accumulated = accumulated * factor[:, :, None] + jnp.einsum(
        "hqk,khd->hqd",
        weights.astype(jnp.bfloat16),
        value_heads,
        preferred_element_type=jnp.float32,
    )
    return (new_max, totals, accumulated)


def empty_state(head_count, row_count):
    return (
        jnp.full((head_count, row_count), low_score, jnp.float32),
        jnp.zeros((head_count, row_count), jnp.float32),
        jnp.zeros((head_count, row_count, HD), jnp.float32),
    )


def visit_block(carry_state, packed, source, query_heads, query_clip, context):
    clip_ends, page_table, page_count, block_total = context
    row_count = query_heads.shape[0]
    head_count = query_heads.shape[1]
    allowed = allowed_keys(
        query_clip, source, clip_ends, page_table, page_count, block_total, row_count
    )
    key_heads = packed[0].reshape(-1, head_count, HD)
    value_heads = packed[1].reshape(-1, head_count, HD)
    return attend(carry_state, query_heads, key_heads, value_heads, allowed)


def gather_row_weight(out_weight, sizes):
    n_zl = sizes["zl"]
    zl = lax.axis_index("zl")
    row_part = jnp.zeros((n_zl,) + out_weight.shape, out_weight.dtype)
    row_part = lax.dynamic_update_index_in_dim(row_part, out_weight, zl, 0)
    for d in range(1, n_zl):
        got = shifted(out_weight, "zl", n_zl, d, wrap=True)
        row_part = lax.dynamic_update_index_in_dim(row_part, got, (zl - d) % n_zl, 0)
    return row_part


def gather_weight(out_weight, sizes, is_first):
    n_y, n_zl = sizes["y"], sizes["zl"]
    rows, cols = out_weight.shape
    other = swap_cores(out_weight)
    pair = jnp.where(
        is_first,
        jnp.concatenate([out_weight, other], axis=0),
        jnp.concatenate([other, out_weight], axis=0),
    )
    zl = lax.axis_index("zl")
    row_block = jnp.zeros((n_zl, 2 * rows, cols), out_weight.dtype)
    row_block = lax.dynamic_update_index_in_dim(row_block, pair, zl, 0)
    for d in range(1, n_zl):
        got = shifted(pair, "zl", n_zl, d, wrap=True)
        row_block = lax.dynamic_update_index_in_dim(row_block, got, (zl - d) % n_zl, 0)
    return row_block.reshape(n_zl * 2 * rows, cols)


def spread_weight(row_block, sizes, is_first):
    n_y = sizes["y"]
    y = lax.axis_index("y")
    cols = row_block.shape[1]
    full = jnp.zeros((n_y,) + row_block.shape, row_block.dtype)
    full = lax.dynamic_update_index_in_dim(full, row_block, y, 0)
    below_count = n_y // 2
    above_count = (n_y - 1) // 2
    received = []
    for j in range(1, below_count + 1):
        route = [(yy * 2, ((yy + j) % n_y) * 2) for yy in range(n_y)]
        if j <= above_count:
            route += [(yy * 2 + 1, ((yy - j) % n_y) * 2 + 1) for yy in range(n_y)]
        received.append(lax.ppermute(row_block, ("y", "c"), route))
    traded = swap_cores(jnp.stack(received))
    for j in range(1, below_count + 1):
        got = received[j - 1]
        if j <= above_count:
            here = jnp.where(is_first, (y - j) % n_y, (y + j) % n_y)
            there = jnp.where(is_first, (y + j) % n_y, (y - j) % n_y)
            full = lax.dynamic_update_index_in_dim(full, got, here, 0)
            full = lax.dynamic_update_index_in_dim(full, traded[j - 1], there, 0)
        else:
            value = jnp.where(is_first, got, traded[j - 1])
            full = lax.dynamic_update_index_in_dim(full, value, (y - j) % n_y, 0)
    return full.reshape(n_y * row_block.shape[0], cols)


def gather_attention(attention_local, sizes):
    n_x = sizes["x"]
    n_tensor = sizes["zh"] * n_x
    row_count, width = attention_local.shape
    zh = lax.axis_index("zh")
    x = lax.axis_index("x")
    partner = lax.ppermute(attention_local, "zh", [(0, 1), (1, 0)])
    both = jnp.where(
        zh == 0,
        jnp.concatenate([attention_local, partner], axis=1),
        jnp.concatenate([partner, attention_local], axis=1),
    )
    pieces = [(both, x)]
    for d in range(1, n_x):
        pieces.append((shifted(both, "x", n_x, d, wrap=True), (x - d) % n_x))
    full = jnp.zeros((row_count, n_tensor * width), attention_local.dtype)
    for piece, piece_x in pieces:
        for half in range(2):
            start = pl_multiple((half * n_x + piece_x) * width)
            full = lax.dynamic_update_slice(
                full, piece[:, half * width:(half + 1) * width], (jnp.int32(0), start)
            )
    return full


def pl_multiple(value):
    return value.astype(jnp.int32)


def make_local(sizes):
    n_chip = sizes["y"] * sizes["zl"]

    def local(
        queries,
        key_tiles,
        value_tiles,
        cache_keys,
        cache_values,
        hidden,
        out_weight,
        gate_table,
        lengths,
        page_table,
        page_count,
        timestep,
    ):
        row_count = queries.shape[0]
        tile_width = queries.shape[1]
        head_count = tile_width // HD
        block_total = n_chip * 2
        chip = lax.axis_index("y") * sizes["zl"] + lax.axis_index("zl")
        core = lax.axis_index("c")
        is_first = core == 0
        seq_index = chip * 2 + core
        clip_ends = jnp.cumsum(lengths, dtype=jnp.int32)
        row_ids = jnp.arange(row_count, dtype=jnp.int32)
        positions = seq_index * row_count + row_ids
        query_clip = clip_index(positions, clip_ends)
        query_heads = queries.reshape(row_count, head_count, HD)
        context = (clip_ends, page_table, page_count, block_total)
        packed = jnp.stack(
            [
                jnp.concatenate([key_tiles, cache_keys.reshape(-1, tile_width)], axis=0),
                jnp.concatenate([value_tiles, cache_values.reshape(-1, tile_width)], axis=0),
            ]
        )
        row_part = gather_row_weight(out_weight, sizes)
        packed, row_part = lax.optimization_barrier((packed, row_part))
        column = lax.all_gather(row_part, "y", axis=0)
        other = swap_cores(column)
        weight_full = jnp.where(
            is_first, jnp.stack([column, other], axis=2), jnp.stack([other, column], axis=2)
        ).reshape(-1, out_weight.shape[1])

        carry_state = visit_block(
            empty_state(head_count, row_count), packed, seq_index, query_heads, query_clip, context
        )
        above = {}
        below = {}
        for d in range(1, 4):
            above[d] = shifted(packed, CHIP, n_chip, -d)
            carry_state = visit_block(
                carry_state, above[d], seq_index + 2 * d, query_heads, query_clip, context
            )
            below[d] = shifted(packed, CHIP, n_chip, d)
            carry_state = visit_block(
                carry_state, below[d], seq_index - 2 * d, query_heads, query_clip, context
            )
        sign = 1 - 2 * core
        got = swap_cores(packed)
        carry_state = visit_block(
            carry_state, got, seq_index + sign, query_heads, query_clip, context
        )
        selected = jnp.where(
            is_first,
            jnp.stack([above[1], above[2], above[3], below[1], below[2]]),
            jnp.stack([below[1], below[2], below[3], above[1], above[2]]),
        )
        traded = swap_cores(selected)
        for slot, offset in enumerate((-1, -3, -5, 3, 5)):
            carry_state = visit_block(
                carry_state, traded[slot], seq_index + sign * offset, query_heads, query_clip, context
            )
        running_max, totals, accumulated = carry_state
        result = accumulated / totals[:, :, None]
        attention_local = (
            jnp.transpose(result, (1, 0, 2)).reshape(row_count, tile_width).astype(jnp.bfloat16)
        )
        attention = gather_attention(attention_local, sizes)
        projected = jnp.dot(attention, weight_full, preferred_element_type=jnp.float32)
        clip_total = lengths.shape[0]
        step_onehot = (
            timestep[:, None] == jnp.arange(gate_table.shape[0], dtype=jnp.int32)[None, :]
        ).astype(jnp.float32)
        clip_gate = jnp.dot(
            step_onehot, gate_table, precision=lax.Precision.HIGHEST, preferred_element_type=jnp.float32
        )
        clip_onehot = (
            query_clip[:, None] == jnp.arange(clip_total, dtype=jnp.int32)[None, :]
        ).astype(jnp.float32)
        token_gate = jnp.dot(
            clip_onehot, clip_gate, precision=lax.Precision.HIGHEST, preferred_element_type=jnp.float32
        )
        return (hidden.astype(jnp.float32) + token_gate * projected).astype(jnp.bfloat16)

    return local


def solution(mesh):
    n_seq = mesh.shape["seq"]
    n_tensor = mesh.shape["tensor"]
    sizes = {"y": n_seq // 8, "zl": 4, "c": 2, "zh": 2, "x": n_tensor // 2}
    devices = np.asarray(mesh.devices).reshape(tuple(sizes[a] for a in AXES))
    fine = Mesh(devices, AXES)
    return jax.shard_map(
        make_local(sizes),
        mesh=fine,
        in_specs=(
            P(SEQ, TENSOR),
            P(SEQ, TENSOR),
            P(SEQ, TENSOR),
            P(SEQ, None, TENSOR),
            P(SEQ, None, TENSOR),
            P(SEQ, TENSOR),
            P(SEQ, TENSOR),
            P(None, TENSOR),
            P(),
            P(),
            P(),
            P(),
        ),
        out_specs=P(SEQ, TENSOR),
        check_vma=False,
    )
```

```python
import math

import numpy as np
import jax
import jax.numpy as jnp
from jax import lax
from jax.sharding import Mesh, PartitionSpec as P

HD = 128
PAGE = 128
POOL = 2
REACH = 6

AXES = ("y", "zl", "c", "zh", "x")
SEQ = ("y", "zl", "c")
TENSOR = ("zh", "x")
CHIP = ("y", "zl")

low_score = -1e30


def shifted(block, axes, size, distance, wrap=False):
    if wrap:
        route = [(i, (i + distance) % size) for i in range(size)]
    else:
        route = [(i, i + distance) for i in range(size) if 0 <= i + distance < size]
    return lax.ppermute(block, axes, route)


def swap_cores(block):
    return lax.ppermute(block, "c", [(0, 1), (1, 0)])


def clip_index(positions, clip_ends):
    return jnp.sum((positions[:, None] >= clip_ends[None, :]).astype(jnp.int32), axis=1)


def allowed_keys(query_clip, source, clip_ends, page_table, page_count, block_total, row_count):
    key_pos = source * row_count + jnp.arange(row_count, dtype=jnp.int32)
    in_range = (source >= 0) & (source < block_total)
    same_clip = (query_clip[:, None] == clip_index(key_pos, clip_ends)[None, :]) & in_range
    clip_total = clip_ends.shape[0]
    page_ids = source * POOL + jnp.arange(POOL, dtype=jnp.int32)
    live_slots = jnp.arange(page_table.shape[1], dtype=jnp.int32)[None, :] < page_count[:, None]
    named_pages = jnp.any(
        live_slots[:, :, None] & (page_table[:, :, None] == page_ids[None, None, :]), axis=1
    )
    member = query_clip[:, None] == jnp.arange(clip_total, dtype=jnp.int32)[None, :]
    page_ok = jnp.any(member[:, :, None] & named_pages[None], axis=1) & in_range
    page_ok = jnp.repeat(page_ok, PAGE, axis=1)
    return jnp.concatenate([same_clip, page_ok], axis=1)


def attend(carry_state, query_heads, key_heads, value_heads, allowed):
    running_max, totals, accumulated = carry_state
    scores = jnp.einsum(
        "qhd,khd->hqk", query_heads, key_heads, preferred_element_type=jnp.float32
    ) * (1.0 / math.sqrt(HD))
    scores = jnp.where(allowed[None], scores, low_score)
    new_max = jnp.maximum(running_max, jnp.max(scores, axis=2))
    factor = jnp.exp(running_max - new_max)
    weights = jnp.where(allowed[None], jnp.exp(scores - new_max[:, :, None]), 0.0)
    totals = totals * factor + jnp.sum(weights, axis=2)
    accumulated = accumulated * factor[:, :, None] + jnp.einsum(
        "hqk,khd->hqd",
        weights.astype(jnp.bfloat16),
        value_heads,
        preferred_element_type=jnp.float32,
    )
    return (new_max, totals, accumulated)


def empty_state(head_count, row_count):
    return (
        jnp.full((head_count, row_count), low_score, jnp.float32),
        jnp.zeros((head_count, row_count), jnp.float32),
        jnp.zeros((head_count, row_count, HD), jnp.float32),
    )


def visit_block(carry_state, packed, source, query_heads, query_clip, context):
    clip_ends, page_table, page_count, block_total = context
    row_count = query_heads.shape[0]
    head_count = query_heads.shape[1]
    allowed = allowed_keys(
        query_clip, source, clip_ends, page_table, page_count, block_total, row_count
    )
    key_heads = packed[0].reshape(-1, head_count, HD)
    value_heads = packed[1].reshape(-1, head_count, HD)
    return attend(carry_state, query_heads, key_heads, value_heads, allowed)


def gather_weight(out_weight, sizes, is_first):
    n_y, n_zl = sizes["y"], sizes["zl"]
    rows, cols = out_weight.shape
    other = swap_cores(out_weight)
    pair = jnp.where(
        is_first,
        jnp.concatenate([out_weight, other], axis=0),
        jnp.concatenate([other, out_weight], axis=0),
    )
    zl = lax.axis_index("zl")
    row_block = jnp.zeros((n_zl, 2 * rows, cols), out_weight.dtype)
    row_block = lax.dynamic_update_index_in_dim(row_block, pair, zl, 0)
    for d in range(1, n_zl):
        got = shifted(pair, "zl", n_zl, d, wrap=True)
        row_block = lax.dynamic_update_index_in_dim(row_block, got, (zl - d) % n_zl, 0)
    return row_block.reshape(n_zl * 2 * rows, cols)


def spread_weight(row_block, sizes, is_first):
    n_y = sizes["y"]
    y = lax.axis_index("y")
    cols = row_block.shape[1]
    full = jnp.zeros((n_y,) + row_block.shape, row_block.dtype)
    full = lax.dynamic_update_index_in_dim(full, row_block, y, 0)
    below_count = n_y // 2
    above_count = (n_y - 1) // 2
    received = []
    for j in range(1, below_count + 1):
        route = [(yy * 2, ((yy + j) % n_y) * 2) for yy in range(n_y)]
        if j <= above_count:
            route += [(yy * 2 + 1, ((yy - j) % n_y) * 2 + 1) for yy in range(n_y)]
        received.append(lax.ppermute(row_block, ("y", "c"), route))
    traded = swap_cores(jnp.stack(received))
    for j in range(1, below_count + 1):
        got = received[j - 1]
        if j <= above_count:
            here = jnp.where(is_first, (y - j) % n_y, (y + j) % n_y)
            there = jnp.where(is_first, (y + j) % n_y, (y - j) % n_y)
            full = lax.dynamic_update_index_in_dim(full, got, here, 0)
            full = lax.dynamic_update_index_in_dim(full, traded[j - 1], there, 0)
        else:
            value = jnp.where(is_first, got, traded[j - 1])
            full = lax.dynamic_update_index_in_dim(full, value, (y - j) % n_y, 0)
    return full.reshape(n_y * row_block.shape[0], cols)


def gather_attention(attention_local, sizes):
    n_x = sizes["x"]
    n_tensor = sizes["zh"] * n_x
    row_count, width = attention_local.shape
    zh = lax.axis_index("zh")
    x = lax.axis_index("x")
    partner = lax.ppermute(attention_local, "zh", [(0, 1), (1, 0)])
    both = jnp.where(
        zh == 0,
        jnp.concatenate([attention_local, partner], axis=1),
        jnp.concatenate([partner, attention_local], axis=1),
    )
    pieces = [(both, x)]
    for d in range(1, n_x):
        pieces.append((shifted(both, "x", n_x, d, wrap=True), (x - d) % n_x))
    full = jnp.zeros((row_count, n_tensor * width), attention_local.dtype)
    for piece, piece_x in pieces:
        for half in range(2):
            start = pl_multiple((half * n_x + piece_x) * width)
            full = lax.dynamic_update_slice(
                full, piece[:, half * width:(half + 1) * width], (jnp.int32(0), start)
            )
    return full


def pl_multiple(value):
    return value.astype(jnp.int32)


def make_local(sizes):
    n_chip = sizes["y"] * sizes["zl"]

    def local(
        queries,
        key_tiles,
        value_tiles,
        cache_keys,
        cache_values,
        hidden,
        out_weight,
        gate_table,
        lengths,
        page_table,
        page_count,
        timestep,
    ):
        row_count = queries.shape[0]
        tile_width = queries.shape[1]
        head_count = tile_width // HD
        block_total = n_chip * 2
        chip = lax.axis_index("y") * sizes["zl"] + lax.axis_index("zl")
        core = lax.axis_index("c")
        is_first = core == 0
        seq_index = chip * 2 + core
        clip_ends = jnp.cumsum(lengths, dtype=jnp.int32)
        row_ids = jnp.arange(row_count, dtype=jnp.int32)
        positions = seq_index * row_count + row_ids
        query_clip = clip_index(positions, clip_ends)
        query_heads = queries.reshape(row_count, head_count, HD)
        context = (clip_ends, page_table, page_count, block_total)
        packed = jnp.stack(
            [
                jnp.concatenate([key_tiles, cache_keys.reshape(-1, tile_width)], axis=0),
                jnp.concatenate([value_tiles, cache_values.reshape(-1, tile_width)], axis=0),
            ]
        )
        row_block = gather_weight(out_weight, sizes, is_first)
        packed, row_block = lax.optimization_barrier((packed, row_block))

        carry_state = visit_block(
            empty_state(head_count, row_count), packed, seq_index, query_heads, query_clip, context
        )
        above = {}
        below = {}
        for d in range(1, 4):
            above[d] = shifted(packed, CHIP, n_chip, -d)
            carry_state = visit_block(
                carry_state, above[d], seq_index + 2 * d, query_heads, query_clip, context
            )
            below[d] = shifted(packed, CHIP, n_chip, d)
            carry_state = visit_block(
                carry_state, below[d], seq_index - 2 * d, query_heads, query_clip, context
            )
        sign = 1 - 2 * core
        gated = lax.optimization_barrier(
            (row_block, above[1], above[2], above[3], below[1], below[2], below[3])
        )
        row_block = gated[0]
        above = dict(zip((1, 2, 3), gated[1:4]))
        below = dict(zip((1, 2, 3), gated[4:7]))
        weight_full = spread_weight(row_block, sizes, is_first)
        got = swap_cores(packed)
        carry_state = visit_block(
            carry_state, got, seq_index + sign, query_heads, query_clip, context
        )
        selected = jnp.where(
            is_first,
            jnp.stack([above[1], above[2], above[3], below[1], below[2]]),
            jnp.stack([below[1], below[2], below[3], above[1], above[2]]),
        )
        traded = swap_cores(selected)
        for slot, offset in enumerate((-1, -3, -5, 3, 5)):
            carry_state = visit_block(
                carry_state, traded[slot], seq_index + sign * offset, query_heads, query_clip, context
            )
        running_max, totals, accumulated = carry_state
        result = accumulated / totals[:, :, None]
        attention_local = (
            jnp.transpose(result, (1, 0, 2)).reshape(row_count, tile_width).astype(jnp.bfloat16)
        )
        attention = gather_attention(attention_local, sizes)
        projected = jnp.dot(attention, weight_full, preferred_element_type=jnp.float32)
        clip_total = lengths.shape[0]
        step_onehot = (
            timestep[:, None] == jnp.arange(gate_table.shape[0], dtype=jnp.int32)[None, :]
        ).astype(jnp.float32)
        clip_gate = jnp.dot(
            step_onehot, gate_table, precision=lax.Precision.HIGHEST, preferred_element_type=jnp.float32
        )
        clip_onehot = (
            query_clip[:, None] == jnp.arange(clip_total, dtype=jnp.int32)[None, :]
        ).astype(jnp.float32)
        token_gate = jnp.dot(
            clip_onehot, clip_gate, precision=lax.Precision.HIGHEST, preferred_element_type=jnp.float32
        )
        return (hidden.astype(jnp.float32) + token_gate * projected).astype(jnp.bfloat16)

    return local


def solution(mesh):
    n_seq = mesh.shape["seq"]
    n_tensor = mesh.shape["tensor"]
    sizes = {"y": n_seq // 8, "zl": 4, "c": 2, "zh": 2, "x": n_tensor // 2}
    devices = np.asarray(mesh.devices).reshape(tuple(sizes[a] for a in AXES))
    fine = Mesh(devices, AXES)
    return jax.shard_map(
        make_local(sizes),
        mesh=fine,
        in_specs=(
            P(SEQ, TENSOR),
            P(SEQ, TENSOR),
            P(SEQ, TENSOR),
            P(SEQ, None, TENSOR),
            P(SEQ, None, TENSOR),
            P(SEQ, TENSOR),
            P(SEQ, TENSOR),
            P(None, TENSOR),
            P(),
            P(),
            P(),
            P(),
        ),
        out_specs=P(SEQ, TENSOR),
        check_vma=False,
    )
```

```python
import math

import numpy as np
import jax
import jax.numpy as jnp
from jax import lax
from jax.sharding import Mesh, PartitionSpec as P

HD = 128
PAGE = 128
POOL = 2
REACH = 6

AXES = ("y", "zl", "c", "zh", "x")
SEQ = ("y", "zl", "c")
TENSOR = ("zh", "x")
CHIP = ("y", "zl")

low_score = -1e30


def shifted(block, axes, size, distance, wrap=False):
    if wrap:
        route = [(i, (i + distance) % size) for i in range(size)]
    else:
        route = [(i, i + distance) for i in range(size) if 0 <= i + distance < size]
    return lax.ppermute(block, axes, route)


def swap_cores(block):
    return lax.ppermute(block, "c", [(0, 1), (1, 0)])


def clip_index(positions, clip_ends):
    return jnp.sum((positions[:, None] >= clip_ends[None, :]).astype(jnp.int32), axis=1)


def allowed_keys(query_clip, source, clip_ends, page_table, page_count, block_total, row_count):
    key_pos = source * row_count + jnp.arange(row_count, dtype=jnp.int32)
    in_range = (source >= 0) & (source < block_total)
    same_clip = (query_clip[:, None] == clip_index(key_pos, clip_ends)[None, :]) & in_range
    clip_total = clip_ends.shape[0]
    page_ids = source * POOL + jnp.arange(POOL, dtype=jnp.int32)
    live_slots = jnp.arange(page_table.shape[1], dtype=jnp.int32)[None, :] < page_count[:, None]
    named_pages = jnp.any(
        live_slots[:, :, None] & (page_table[:, :, None] == page_ids[None, None, :]), axis=1
    )
    member = query_clip[:, None] == jnp.arange(clip_total, dtype=jnp.int32)[None, :]
    page_ok = jnp.any(member[:, :, None] & named_pages[None], axis=1) & in_range
    page_ok = jnp.repeat(page_ok, PAGE, axis=1)
    return jnp.concatenate([same_clip, page_ok], axis=1)


def attend(carry_state, query_heads, key_heads, value_heads, allowed):
    running_max, totals, accumulated = carry_state
    scores = jnp.einsum(
        "qhd,khd->hqk", query_heads, key_heads, preferred_element_type=jnp.float32
    ) * (1.0 / math.sqrt(HD))
    scores = jnp.where(allowed[None], scores, low_score)
    new_max = jnp.maximum(running_max, jnp.max(scores, axis=2))
    factor = jnp.exp(running_max - new_max)
    weights = jnp.where(allowed[None], jnp.exp(scores - new_max[:, :, None]), 0.0)
    totals = totals * factor + jnp.sum(weights, axis=2)
    accumulated = accumulated * factor[:, :, None] + jnp.einsum(
        "hqk,khd->hqd",
        weights.astype(jnp.bfloat16),
        value_heads,
        preferred_element_type=jnp.float32,
    )
    return (new_max, totals, accumulated)


def empty_state(head_count, row_count):
    return (
        jnp.full((head_count, row_count), low_score, jnp.float32),
        jnp.zeros((head_count, row_count), jnp.float32),
        jnp.zeros((head_count, row_count, HD), jnp.float32),
    )


def visit_block(carry_state, packed, source, query_heads, query_clip, context):
    clip_ends, page_table, page_count, block_total = context
    row_count = query_heads.shape[0]
    head_count = query_heads.shape[1]
    allowed = allowed_keys(
        query_clip, source, clip_ends, page_table, page_count, block_total, row_count
    )
    key_heads = packed[0].reshape(-1, head_count, HD)
    value_heads = packed[1].reshape(-1, head_count, HD)
    return attend(carry_state, query_heads, key_heads, value_heads, allowed)


def gather_weight(out_weight, sizes, is_first):
    n_y, n_zl = sizes["y"], sizes["zl"]
    rows, cols = out_weight.shape
    other = swap_cores(out_weight)
    pair = jnp.where(
        is_first,
        jnp.concatenate([out_weight, other], axis=0),
        jnp.concatenate([other, out_weight], axis=0),
    )
    zl = lax.axis_index("zl")
    row_block = jnp.zeros((n_zl, 2 * rows, cols), out_weight.dtype)
    row_block = lax.dynamic_update_index_in_dim(row_block, pair, zl, 0)
    for d in range(1, n_zl):
        got = shifted(pair, "zl", n_zl, d, wrap=True)
        row_block = lax.dynamic_update_index_in_dim(row_block, got, (zl - d) % n_zl, 0)
    return row_block.reshape(n_zl * 2 * rows, cols)


def spread_weight(row_block, sizes, is_first):
    n_y = sizes["y"]
    y = lax.axis_index("y")
    cols = row_block.shape[1]
    full = jnp.zeros((n_y,) + row_block.shape, row_block.dtype)
    full = lax.dynamic_update_index_in_dim(full, row_block, y, 0)
    below_count = n_y // 2
    above_count = (n_y - 1) // 2
    received = []
    for j in range(1, below_count + 1):
        route = [(yy * 2, ((yy + j) % n_y) * 2) for yy in range(n_y)]
        if j <= above_count:
            route += [(yy * 2 + 1, ((yy - j) % n_y) * 2 + 1) for yy in range(n_y)]
        received.append(lax.ppermute(row_block, ("y", "c"), route))
    traded = swap_cores(jnp.stack(received))
    for j in range(1, below_count + 1):
        got = received[j - 1]
        if j <= above_count:
            here = jnp.where(is_first, (y - j) % n_y, (y + j) % n_y)
            there = jnp.where(is_first, (y + j) % n_y, (y - j) % n_y)
            full = lax.dynamic_update_index_in_dim(full, got, here, 0)
            full = lax.dynamic_update_index_in_dim(full, traded[j - 1], there, 0)
        else:
            value = jnp.where(is_first, got, traded[j - 1])
            full = lax.dynamic_update_index_in_dim(full, value, (y - j) % n_y, 0)
    return full.reshape(n_y * row_block.shape[0], cols)


def gather_attention(attention_local, sizes):
    n_x = sizes["x"]
    n_tensor = sizes["zh"] * n_x
    row_count, width = attention_local.shape
    zh = lax.axis_index("zh")
    x = lax.axis_index("x")
    partner = lax.ppermute(attention_local, "zh", [(0, 1), (1, 0)])
    both = jnp.where(
        zh == 0,
        jnp.concatenate([attention_local, partner], axis=1),
        jnp.concatenate([partner, attention_local], axis=1),
    )
    pieces = [(both, x)]
    for d in range(1, n_x):
        pieces.append((shifted(both, "x", n_x, d, wrap=True), (x - d) % n_x))
    full = jnp.zeros((row_count, n_tensor * width), attention_local.dtype)
    for piece, piece_x in pieces:
        for half in range(2):
            start = pl_multiple((half * n_x + piece_x) * width)
            full = lax.dynamic_update_slice(
                full, piece[:, half * width:(half + 1) * width], (jnp.int32(0), start)
            )
    return full


def pl_multiple(value):
    return value.astype(jnp.int32)


def make_local(sizes):
    n_chip = sizes["y"] * sizes["zl"]

    def local(
        queries,
        key_tiles,
        value_tiles,
        cache_keys,
        cache_values,
        hidden,
        out_weight,
        gate_table,
        lengths,
        page_table,
        page_count,
        timestep,
    ):
        row_count = queries.shape[0]
        tile_width = queries.shape[1]
        head_count = tile_width // HD
        block_total = n_chip * 2
        chip = lax.axis_index("y") * sizes["zl"] + lax.axis_index("zl")
        core = lax.axis_index("c")
        is_first = core == 0
        seq_index = chip * 2 + core
        clip_ends = jnp.cumsum(lengths, dtype=jnp.int32)
        row_ids = jnp.arange(row_count, dtype=jnp.int32)
        positions = seq_index * row_count + row_ids
        query_clip = clip_index(positions, clip_ends)
        query_heads = queries.reshape(row_count, head_count, HD)
        context = (clip_ends, page_table, page_count, block_total)
        packed = jnp.stack(
            [
                jnp.concatenate([key_tiles, cache_keys.reshape(-1, tile_width)], axis=0),
                jnp.concatenate([value_tiles, cache_values.reshape(-1, tile_width)], axis=0),
            ]
        )
        sign = 1 - 2 * core
        own_pair = swap_cores(packed)
        row_block = gather_weight(out_weight, sizes, is_first)
        packed, row_block, own_pair = lax.optimization_barrier((packed, row_block, own_pair))
        weight_full = spread_weight(row_block, sizes, is_first)

        carry_state = visit_block(
            empty_state(head_count, row_count), packed, seq_index, query_heads, query_clip, context
        )
        carry_state = visit_block(
            carry_state, own_pair, seq_index + sign, query_heads, query_clip, context
        )
        above = {}
        below = {}
        for d in range(1, 4):
            above[d] = shifted(packed, CHIP, n_chip, -d)
            carry_state = visit_block(
                carry_state, above[d], seq_index + 2 * d, query_heads, query_clip, context
            )
            below[d] = shifted(packed, CHIP, n_chip, d)
            carry_state = visit_block(
                carry_state, below[d], seq_index - 2 * d, query_heads, query_clip, context
            )
        selected = jnp.where(
            is_first,
            jnp.stack([above[1], above[2], above[3], below[1], below[2]]),
            jnp.stack([below[1], below[2], below[3], above[1], above[2]]),
        )
        traded = swap_cores(selected)
        for slot, offset in enumerate((-1, -3, -5, 3, 5)):
            carry_state = visit_block(
                carry_state, traded[slot], seq_index + sign * offset, query_heads, query_clip, context
            )
        running_max, totals, accumulated = carry_state
        result = accumulated / totals[:, :, None]
        attention_local = (
            jnp.transpose(result, (1, 0, 2)).reshape(row_count, tile_width).astype(jnp.bfloat16)
        )
        attention = gather_attention(attention_local, sizes)
        projected = jnp.dot(attention, weight_full, preferred_element_type=jnp.float32)
        clip_total = lengths.shape[0]
        step_onehot = (
            timestep[:, None] == jnp.arange(gate_table.shape[0], dtype=jnp.int32)[None, :]
        ).astype(jnp.float32)
        clip_gate = jnp.dot(
            step_onehot, gate_table, precision=lax.Precision.HIGHEST, preferred_element_type=jnp.float32
        )
        clip_onehot = (
            query_clip[:, None] == jnp.arange(clip_total, dtype=jnp.int32)[None, :]
        ).astype(jnp.float32)
        token_gate = jnp.dot(
            clip_onehot, clip_gate, precision=lax.Precision.HIGHEST, preferred_element_type=jnp.float32
        )
        return (hidden.astype(jnp.float32) + token_gate * projected).astype(jnp.bfloat16)

    return local


def solution(mesh):
    n_seq = mesh.shape["seq"]
    n_tensor = mesh.shape["tensor"]
    sizes = {"y": n_seq // 8, "zl": 4, "c": 2, "zh": 2, "x": n_tensor // 2}
    devices = np.asarray(mesh.devices).reshape(tuple(sizes[a] for a in AXES))
    fine = Mesh(devices, AXES)
    return jax.shard_map(
        make_local(sizes),
        mesh=fine,
        in_specs=(
            P(SEQ, TENSOR),
            P(SEQ, TENSOR),
            P(SEQ, TENSOR),
            P(SEQ, None, TENSOR),
            P(SEQ, None, TENSOR),
            P(SEQ, TENSOR),
            P(SEQ, TENSOR),
            P(None, TENSOR),
            P(),
            P(),
            P(),
            P(),
        ),
        out_specs=P(SEQ, TENSOR),
        check_vma=False,
    )
```

```python
import math

import numpy as np
import jax
import jax.numpy as jnp
from jax import lax
from jax.sharding import Mesh, PartitionSpec as P

HD = 128
PAGE = 128
POOL = 2
REACH = 6

AXES = ("y", "zl", "c", "zh", "x")
SEQ = ("y", "zl", "c")
TENSOR = ("zh", "x")
CHIP = ("y", "zl")

low_score = -1e30


def shifted(block, axes, size, distance, wrap=False):
    if wrap:
        route = [(i, (i + distance) % size) for i in range(size)]
    else:
        route = [(i, i + distance) for i in range(size) if 0 <= i + distance < size]
    return lax.ppermute(block, axes, route)


def swap_cores(block):
    return lax.ppermute(block, "c", [(0, 1), (1, 0)])


def clip_index(positions, clip_ends):
    return jnp.sum((positions[:, None] >= clip_ends[None, :]).astype(jnp.int32), axis=1)


def allowed_keys(query_clip, source, clip_ends, page_table, page_count, block_total, row_count):
    key_pos = source * row_count + jnp.arange(row_count, dtype=jnp.int32)
    in_range = (source >= 0) & (source < block_total)
    same_clip = (query_clip[:, None] == clip_index(key_pos, clip_ends)[None, :]) & in_range
    clip_total = clip_ends.shape[0]
    page_ids = source * POOL + jnp.arange(POOL, dtype=jnp.int32)
    live_slots = jnp.arange(page_table.shape[1], dtype=jnp.int32)[None, :] < page_count[:, None]
    named_pages = jnp.any(
        live_slots[:, :, None] & (page_table[:, :, None] == page_ids[None, None, :]), axis=1
    )
    member = query_clip[:, None] == jnp.arange(clip_total, dtype=jnp.int32)[None, :]
    page_ok = jnp.any(member[:, :, None] & named_pages[None], axis=1) & in_range
    page_ok = jnp.repeat(page_ok, PAGE, axis=1)
    return jnp.concatenate([same_clip, page_ok], axis=1)


def attend(carry_state, query_heads, key_heads, value_heads, allowed):
    running_max, totals, accumulated = carry_state
    scores = jnp.einsum(
        "qhd,khd->hqk", query_heads, key_heads, preferred_element_type=jnp.float32
    ) * (1.0 / math.sqrt(HD))
    scores = jnp.where(allowed[None], scores, low_score)
    new_max = jnp.maximum(running_max, jnp.max(scores, axis=2))
    factor = jnp.exp(running_max - new_max)
    weights = jnp.where(allowed[None], jnp.exp(scores - new_max[:, :, None]), 0.0)
    totals = totals * factor + jnp.sum(weights, axis=2)
    accumulated = accumulated * factor[:, :, None] + jnp.einsum(
        "hqk,khd->hqd",
        weights.astype(jnp.bfloat16),
        value_heads,
        preferred_element_type=jnp.float32,
    )
    return (new_max, totals, accumulated)


def empty_state(head_count, row_count):
    return (
        jnp.full((head_count, row_count), low_score, jnp.float32),
        jnp.zeros((head_count, row_count), jnp.float32),
        jnp.zeros((head_count, row_count, HD), jnp.float32),
    )


def visit_block(carry_state, packed, source, query_heads, query_clip, context):
    clip_ends, page_table, page_count, block_total = context
    row_count = query_heads.shape[0]
    head_count = query_heads.shape[1]
    allowed = allowed_keys(
        query_clip, source, clip_ends, page_table, page_count, block_total, row_count
    )
    key_heads = packed[0].reshape(-1, head_count, HD)
    value_heads = packed[1].reshape(-1, head_count, HD)
    return attend(carry_state, query_heads, key_heads, value_heads, allowed)


def gather_weight(out_weight, sizes, is_first):
    n_y, n_zl = sizes["y"], sizes["zl"]
    rows, cols = out_weight.shape
    other = swap_cores(out_weight)
    pair = jnp.where(
        is_first,
        jnp.concatenate([out_weight, other], axis=0),
        jnp.concatenate([other, out_weight], axis=0),
    )
    zl = lax.axis_index("zl")
    row_block = jnp.zeros((n_zl, 2 * rows, cols), out_weight.dtype)
    row_block = lax.dynamic_update_index_in_dim(row_block, pair, zl, 0)
    for d in range(1, n_zl):
        got = shifted(pair, "zl", n_zl, d, wrap=True)
        row_block = lax.dynamic_update_index_in_dim(row_block, got, (zl - d) % n_zl, 0)
    return row_block.reshape(n_zl * 2 * rows, cols)


def spread_weight(row_block, sizes, is_first):
    n_y = sizes["y"]
    y = lax.axis_index("y")
    cols = row_block.shape[1]
    full = jnp.zeros((n_y,) + row_block.shape, row_block.dtype)
    full = lax.dynamic_update_index_in_dim(full, row_block, y, 0)
    below_count = n_y // 2
    above_count = (n_y - 1) // 2
    received = []
    for j in range(1, below_count + 1):
        route = [(yy * 2, ((yy + j) % n_y) * 2) for yy in range(n_y)]
        if j <= above_count:
            route += [(yy * 2 + 1, ((yy - j) % n_y) * 2 + 1) for yy in range(n_y)]
        received.append(lax.ppermute(row_block, ("y", "c"), route))
    traded = swap_cores(jnp.stack(received))
    for j in range(1, below_count + 1):
        got = received[j - 1]
        if j <= above_count:
            here = jnp.where(is_first, (y - j) % n_y, (y + j) % n_y)
            there = jnp.where(is_first, (y + j) % n_y, (y - j) % n_y)
            full = lax.dynamic_update_index_in_dim(full, got, here, 0)
            full = lax.dynamic_update_index_in_dim(full, traded[j - 1], there, 0)
        else:
            value = jnp.where(is_first, got, traded[j - 1])
            full = lax.dynamic_update_index_in_dim(full, value, (y - j) % n_y, 0)
    return full.reshape(n_y * row_block.shape[0], cols)


def gather_attention(attention_local, sizes):
    n_x = sizes["x"]
    n_tensor = sizes["zh"] * n_x
    row_count, width = attention_local.shape
    zh = lax.axis_index("zh")
    x = lax.axis_index("x")
    partner = lax.ppermute(attention_local, "zh", [(0, 1), (1, 0)])
    both = jnp.where(
        zh == 0,
        jnp.concatenate([attention_local, partner], axis=1),
        jnp.concatenate([partner, attention_local], axis=1),
    )
    pieces = [(both, x)]
    for d in range(1, n_x):
        pieces.append((shifted(both, "x", n_x, d, wrap=True), (x - d) % n_x))
    full = jnp.zeros((row_count, n_tensor * width), attention_local.dtype)
    for piece, piece_x in pieces:
        for half in range(2):
            start = pl_multiple((half * n_x + piece_x) * width)
            full = lax.dynamic_update_slice(
                full, piece[:, half * width:(half + 1) * width], (jnp.int32(0), start)
            )
    return full


def pl_multiple(value):
    return value.astype(jnp.int32)


def make_local(sizes):
    n_chip = sizes["y"] * sizes["zl"]

    def local(
        queries,
        key_tiles,
        value_tiles,
        cache_keys,
        cache_values,
        hidden,
        out_weight,
        gate_table,
        lengths,
        page_table,
        page_count,
        timestep,
    ):
        row_count = queries.shape[0]
        tile_width = queries.shape[1]
        head_count = tile_width // HD
        block_total = n_chip * 2
        chip = lax.axis_index("y") * sizes["zl"] + lax.axis_index("zl")
        core = lax.axis_index("c")
        is_first = core == 0
        seq_index = chip * 2 + core
        clip_ends = jnp.cumsum(lengths, dtype=jnp.int32)
        row_ids = jnp.arange(row_count, dtype=jnp.int32)
        positions = seq_index * row_count + row_ids
        query_clip = clip_index(positions, clip_ends)
        query_heads = queries.reshape(row_count, head_count, HD)
        context = (clip_ends, page_table, page_count, block_total)
        packed = jnp.stack(
            [
                jnp.concatenate([key_tiles, cache_keys.reshape(-1, tile_width)], axis=0),
                jnp.concatenate([value_tiles, cache_values.reshape(-1, tile_width)], axis=0),
            ]
        )
        sign = 1 - 2 * core
        own_pair = swap_cores(packed)
        row_block = gather_weight(out_weight, sizes, is_first)
        packed, row_block, own_pair = lax.optimization_barrier((packed, row_block, own_pair))
        weight_full = spread_weight(row_block, sizes, is_first)

        carry_state = visit_block(
            empty_state(head_count, row_count), packed, seq_index, query_heads, query_clip, context
        )
        carry_state = visit_block(
            carry_state, own_pair, seq_index + sign, query_heads, query_clip, context
        )
        above = {}
        below = {}
        for d in range(1, 4):
            above[d] = shifted(packed, CHIP, n_chip, -d)
            carry_state = visit_block(
                carry_state, above[d], seq_index + 2 * d, query_heads, query_clip, context
            )
            below[d] = shifted(packed, CHIP, n_chip, d)
            carry_state = visit_block(
                carry_state, below[d], seq_index - 2 * d, query_heads, query_clip, context
            )
        near = swap_cores(
            jnp.where(
                is_first,
                jnp.stack([above[1], above[2], below[1], below[2]]),
                jnp.stack([below[1], below[2], above[1], above[2]]),
            )
        )
        for slot, offset in enumerate((-1, -3, 3, 5)):
            carry_state = visit_block(
                carry_state, near[slot], seq_index + sign * offset, query_heads, query_clip, context
            )
        far = swap_cores(jnp.where(is_first, above[3], below[3]))
        carry_state = visit_block(
            carry_state, far, seq_index - sign * 5, query_heads, query_clip, context
        )
        running_max, totals, accumulated = carry_state
        result = accumulated / totals[:, :, None]
        attention_local = (
            jnp.transpose(result, (1, 0, 2)).reshape(row_count, tile_width).astype(jnp.bfloat16)
        )
        attention = gather_attention(attention_local, sizes)
        projected = jnp.dot(attention, weight_full, preferred_element_type=jnp.float32)
        clip_total = lengths.shape[0]
        step_onehot = (
            timestep[:, None] == jnp.arange(gate_table.shape[0], dtype=jnp.int32)[None, :]
        ).astype(jnp.float32)
        clip_gate = jnp.dot(
            step_onehot, gate_table, precision=lax.Precision.HIGHEST, preferred_element_type=jnp.float32
        )
        clip_onehot = (
            query_clip[:, None] == jnp.arange(clip_total, dtype=jnp.int32)[None, :]
        ).astype(jnp.float32)
        token_gate = jnp.dot(
            clip_onehot, clip_gate, precision=lax.Precision.HIGHEST, preferred_element_type=jnp.float32
        )
        return (hidden.astype(jnp.float32) + token_gate * projected).astype(jnp.bfloat16)

    return local


def solution(mesh):
    n_seq = mesh.shape["seq"]
    n_tensor = mesh.shape["tensor"]
    sizes = {"y": n_seq // 8, "zl": 4, "c": 2, "zh": 2, "x": n_tensor // 2}
    devices = np.asarray(mesh.devices).reshape(tuple(sizes[a] for a in AXES))
    fine = Mesh(devices, AXES)
    return jax.shard_map(
        make_local(sizes),
        mesh=fine,
        in_specs=(
            P(SEQ, TENSOR),
            P(SEQ, TENSOR),
            P(SEQ, TENSOR),
            P(SEQ, None, TENSOR),
            P(SEQ, None, TENSOR),
            P(SEQ, TENSOR),
            P(SEQ, TENSOR),
            P(None, TENSOR),
            P(),
            P(),
            P(),
            P(),
        ),
        out_specs=P(SEQ, TENSOR),
        check_vma=False,
    )
```

```python
import math

import numpy as np
import jax
import jax.numpy as jnp
from jax import lax
from jax.sharding import Mesh, PartitionSpec as P

HD = 128
PAGE = 128
POOL = 2
REACH = 6

AXES = ("y", "zl", "c", "zh", "x")
SEQ = ("y", "zl", "c")
TENSOR = ("zh", "x")
CHIP = ("y", "zl")

low_score = -1e30


def shifted(block, axes, size, distance, wrap=False):
    if wrap:
        route = [(i, (i + distance) % size) for i in range(size)]
    else:
        route = [(i, i + distance) for i in range(size) if 0 <= i + distance < size]
    return lax.ppermute(block, axes, route)


def swap_cores(block):
    return lax.ppermute(block, "c", [(0, 1), (1, 0)])


def clip_index(positions, clip_ends):
    return jnp.sum((positions[:, None] >= clip_ends[None, :]).astype(jnp.int32), axis=1)


def allowed_keys(query_clip, source, clip_ends, page_table, page_count, block_total, row_count):
    key_pos = source * row_count + jnp.arange(row_count, dtype=jnp.int32)
    in_range = (source >= 0) & (source < block_total)
    same_clip = (query_clip[:, None] == clip_index(key_pos, clip_ends)[None, :]) & in_range
    clip_total = clip_ends.shape[0]
    page_ids = source * POOL + jnp.arange(POOL, dtype=jnp.int32)
    live_slots = jnp.arange(page_table.shape[1], dtype=jnp.int32)[None, :] < page_count[:, None]
    named_pages = jnp.any(
        live_slots[:, :, None] & (page_table[:, :, None] == page_ids[None, None, :]), axis=1
    )
    member = query_clip[:, None] == jnp.arange(clip_total, dtype=jnp.int32)[None, :]
    page_ok = jnp.any(member[:, :, None] & named_pages[None], axis=1) & in_range
    page_ok = jnp.repeat(page_ok, PAGE, axis=1)
    return jnp.concatenate([same_clip, page_ok], axis=1)


def attend(carry_state, query_heads, key_heads, value_heads, allowed):
    running_max, totals, accumulated = carry_state
    scores = jnp.einsum(
        "qhd,khd->hqk", query_heads, key_heads, preferred_element_type=jnp.float32
    ) * (1.0 / math.sqrt(HD))
    scores = jnp.where(allowed[None], scores, low_score)
    new_max = jnp.maximum(running_max, jnp.max(scores, axis=2))
    factor = jnp.exp(running_max - new_max)
    weights = jnp.where(allowed[None], jnp.exp(scores - new_max[:, :, None]), 0.0)
    totals = totals * factor + jnp.sum(weights, axis=2)
    accumulated = accumulated * factor[:, :, None] + jnp.einsum(
        "hqk,khd->hqd",
        weights.astype(jnp.bfloat16),
        value_heads,
        preferred_element_type=jnp.float32,
    )
    return (new_max, totals, accumulated)


def empty_state(head_count, row_count):
    return (
        jnp.full((head_count, row_count), low_score, jnp.float32),
        jnp.zeros((head_count, row_count), jnp.float32),
        jnp.zeros((head_count, row_count, HD), jnp.float32),
    )


def visit_block(carry_state, packed, source, query_heads, query_clip, context):
    clip_ends, page_table, page_count, block_total = context
    row_count = query_heads.shape[0]
    head_count = query_heads.shape[1]
    allowed = allowed_keys(
        query_clip, source, clip_ends, page_table, page_count, block_total, row_count
    )
    key_heads = packed[0].reshape(-1, head_count, HD)
    value_heads = packed[1].reshape(-1, head_count, HD)
    return attend(carry_state, query_heads, key_heads, value_heads, allowed)


def gather_weight(out_weight, sizes, is_first):
    n_y, n_zl = sizes["y"], sizes["zl"]
    rows, cols = out_weight.shape
    other = swap_cores(out_weight)
    pair = jnp.where(
        is_first,
        jnp.concatenate([out_weight, other], axis=0),
        jnp.concatenate([other, out_weight], axis=0),
    )
    zl = lax.axis_index("zl")
    row_block = jnp.zeros((n_zl, 2 * rows, cols), out_weight.dtype)
    row_block = lax.dynamic_update_index_in_dim(row_block, pair, zl, 0)
    for d in range(1, n_zl):
        got = shifted(pair, "zl", n_zl, d, wrap=True)
        row_block = lax.dynamic_update_index_in_dim(row_block, got, (zl - d) % n_zl, 0)
    return row_block.reshape(n_zl * 2 * rows, cols)


def spread_weight(row_block, sizes, is_first):
    n_y = sizes["y"]
    y = lax.axis_index("y")
    cols = row_block.shape[1]
    full = jnp.zeros((n_y,) + row_block.shape, row_block.dtype)
    full = lax.dynamic_update_index_in_dim(full, row_block, y, 0)
    below_count = n_y // 2
    above_count = (n_y - 1) // 2
    received = []
    for j in range(1, below_count + 1):
        route = [(yy * 2, ((yy + j) % n_y) * 2) for yy in range(n_y)]
        if j <= above_count:
            route += [(yy * 2 + 1, ((yy - j) % n_y) * 2 + 1) for yy in range(n_y)]
        received.append(lax.ppermute(row_block, ("y", "c"), route))
    traded = swap_cores(jnp.stack(received))
    for j in range(1, below_count + 1):
        got = received[j - 1]
        if j <= above_count:
            here = jnp.where(is_first, (y - j) % n_y, (y + j) % n_y)
            there = jnp.where(is_first, (y + j) % n_y, (y - j) % n_y)
            full = lax.dynamic_update_index_in_dim(full, got, here, 0)
            full = lax.dynamic_update_index_in_dim(full, traded[j - 1], there, 0)
        else:
            value = jnp.where(is_first, got, traded[j - 1])
            full = lax.dynamic_update_index_in_dim(full, value, (y - j) % n_y, 0)
    return full.reshape(n_y * row_block.shape[0], cols)


def gather_attention(attention_local, sizes):
    n_x = sizes["x"]
    n_tensor = sizes["zh"] * n_x
    row_count, width = attention_local.shape
    zh = lax.axis_index("zh")
    x = lax.axis_index("x")
    partner = lax.ppermute(attention_local, "zh", [(0, 1), (1, 0)])
    both = jnp.where(
        zh == 0,
        jnp.concatenate([attention_local, partner], axis=1),
        jnp.concatenate([partner, attention_local], axis=1),
    )
    pieces = [(both, x)]
    for d in range(1, n_x):
        pieces.append((shifted(both, "x", n_x, d, wrap=True), (x - d) % n_x))
    full = jnp.zeros((row_count, n_tensor * width), attention_local.dtype)
    for piece, piece_x in pieces:
        for half in range(2):
            start = pl_multiple((half * n_x + piece_x) * width)
            full = lax.dynamic_update_slice(
                full, piece[:, half * width:(half + 1) * width], (jnp.int32(0), start)
            )
    return full


def pl_multiple(value):
    return value.astype(jnp.int32)


def make_local(sizes):
    n_chip = sizes["y"] * sizes["zl"]

    def local(
        queries,
        key_tiles,
        value_tiles,
        cache_keys,
        cache_values,
        hidden,
        out_weight,
        gate_table,
        lengths,
        page_table,
        page_count,
        timestep,
    ):
        row_count = queries.shape[0]
        tile_width = queries.shape[1]
        head_count = tile_width // HD
        block_total = n_chip * 2
        chip = lax.axis_index("y") * sizes["zl"] + lax.axis_index("zl")
        core = lax.axis_index("c")
        is_first = core == 0
        seq_index = chip * 2 + core
        clip_ends = jnp.cumsum(lengths, dtype=jnp.int32)
        row_ids = jnp.arange(row_count, dtype=jnp.int32)
        positions = seq_index * row_count + row_ids
        query_clip = clip_index(positions, clip_ends)
        query_heads = queries.reshape(row_count, head_count, HD)
        context = (clip_ends, page_table, page_count, block_total)
        packed = jnp.stack(
            [
                jnp.concatenate([key_tiles, cache_keys.reshape(-1, tile_width)], axis=0),
                jnp.concatenate([value_tiles, cache_values.reshape(-1, tile_width)], axis=0),
            ]
        )
        sign = 1 - 2 * core
        own_pair = swap_cores(packed)
        row_block = gather_weight(out_weight, sizes, is_first)
        packed, own_pair = lax.optimization_barrier((packed, own_pair))
        weight_full = spread_weight(row_block, sizes, is_first)

        carry_state = visit_block(
            empty_state(head_count, row_count), packed, seq_index, query_heads, query_clip, context
        )
        carry_state = visit_block(
            carry_state, own_pair, seq_index + sign, query_heads, query_clip, context
        )
        above = {}
        below = {}
        for d in range(1, 4):
            above[d] = shifted(packed, CHIP, n_chip, -d)
            carry_state = visit_block(
                carry_state, above[d], seq_index + 2 * d, query_heads, query_clip, context
            )
            below[d] = shifted(packed, CHIP, n_chip, d)
            carry_state = visit_block(
                carry_state, below[d], seq_index - 2 * d, query_heads, query_clip, context
            )
        selected = jnp.where(
            is_first,
            jnp.stack([above[1], above[2], above[3], below[1], below[2]]),
            jnp.stack([below[1], below[2], below[3], above[1], above[2]]),
        )
        traded = swap_cores(selected)
        for slot, offset in enumerate((-1, -3, -5, 3, 5)):
            carry_state = visit_block(
                carry_state, traded[slot], seq_index + sign * offset, query_heads, query_clip, context
            )
        running_max, totals, accumulated = carry_state
        result = accumulated / totals[:, :, None]
        attention_local = (
            jnp.transpose(result, (1, 0, 2)).reshape(row_count, tile_width).astype(jnp.bfloat16)
        )
        attention = gather_attention(attention_local, sizes)
        projected = jnp.dot(attention, weight_full, preferred_element_type=jnp.float32)
        clip_total = lengths.shape[0]
        step_onehot = (
            timestep[:, None] == jnp.arange(gate_table.shape[0], dtype=jnp.int32)[None, :]
        ).astype(jnp.float32)
        clip_gate = jnp.dot(
            step_onehot, gate_table, precision=lax.Precision.HIGHEST, preferred_element_type=jnp.float32
        )
        clip_onehot = (
            query_clip[:, None] == jnp.arange(clip_total, dtype=jnp.int32)[None, :]
        ).astype(jnp.float32)
        token_gate = jnp.dot(
            clip_onehot, clip_gate, precision=lax.Precision.HIGHEST, preferred_element_type=jnp.float32
        )
        return (hidden.astype(jnp.float32) + token_gate * projected).astype(jnp.bfloat16)

    return local


def solution(mesh):
    n_seq = mesh.shape["seq"]
    n_tensor = mesh.shape["tensor"]
    sizes = {"y": n_seq // 8, "zl": 4, "c": 2, "zh": 2, "x": n_tensor // 2}
    devices = np.asarray(mesh.devices).reshape(tuple(sizes[a] for a in AXES))
    fine = Mesh(devices, AXES)
    return jax.shard_map(
        make_local(sizes),
        mesh=fine,
        in_specs=(
            P(SEQ, TENSOR),
            P(SEQ, TENSOR),
            P(SEQ, TENSOR),
            P(SEQ, None, TENSOR),
            P(SEQ, None, TENSOR),
            P(SEQ, TENSOR),
            P(SEQ, TENSOR),
            P(None, TENSOR),
            P(),
            P(),
            P(),
            P(),
        ),
        out_specs=P(SEQ, TENSOR),
        check_vma=False,
    )
```

```python
import math

import numpy as np
import jax
import jax.numpy as jnp
from jax import lax
from jax.sharding import Mesh, PartitionSpec as P

HD = 128
PAGE = 128
POOL = 2
REACH = 6

AXES = ("y", "zl", "c", "zh", "x")
SEQ = ("y", "zl", "c")
TENSOR = ("zh", "x")
CHIP = ("y", "zl")

low_score = -1e30


def shifted(block, axes, size, distance, wrap=False):
    if wrap:
        route = [(i, (i + distance) % size) for i in range(size)]
    else:
        route = [(i, i + distance) for i in range(size) if 0 <= i + distance < size]
    return lax.ppermute(block, axes, route)


def swap_cores(block):
    return lax.ppermute(block, "c", [(0, 1), (1, 0)])


def clip_index(positions, clip_ends):
    return jnp.sum((positions[:, None] >= clip_ends[None, :]).astype(jnp.int32), axis=1)


def allowed_keys(query_clip, source, clip_ends, page_table, page_count, block_total, row_count):
    key_pos = source * row_count + jnp.arange(row_count, dtype=jnp.int32)
    in_range = (source >= 0) & (source < block_total)
    same_clip = (query_clip[:, None] == clip_index(key_pos, clip_ends)[None, :]) & in_range
    clip_total = clip_ends.shape[0]
    page_ids = source * POOL + jnp.arange(POOL, dtype=jnp.int32)
    live_slots = jnp.arange(page_table.shape[1], dtype=jnp.int32)[None, :] < page_count[:, None]
    named_pages = jnp.any(
        live_slots[:, :, None] & (page_table[:, :, None] == page_ids[None, None, :]), axis=1
    )
    member = query_clip[:, None] == jnp.arange(clip_total, dtype=jnp.int32)[None, :]
    page_ok = jnp.any(member[:, :, None] & named_pages[None], axis=1) & in_range
    page_ok = jnp.repeat(page_ok, PAGE, axis=1)
    return jnp.concatenate([same_clip, page_ok], axis=1)


def attend(carry_state, query_heads, key_heads, value_heads, allowed):
    running_max, totals, accumulated = carry_state
    scores = jnp.einsum(
        "qhd,khd->hqk", query_heads, key_heads, preferred_element_type=jnp.float32
    ) * (1.0 / math.sqrt(HD))
    scores = jnp.where(allowed[None], scores, low_score)
    new_max = jnp.maximum(running_max, jnp.max(scores, axis=2))
    factor = jnp.exp(running_max - new_max)
    weights = jnp.where(allowed[None], jnp.exp(scores - new_max[:, :, None]), 0.0)
    totals = totals * factor + jnp.sum(weights, axis=2)
    accumulated = accumulated * factor[:, :, None] + jnp.einsum(
        "hqk,khd->hqd",
        weights.astype(jnp.bfloat16),
        value_heads,
        preferred_element_type=jnp.float32,
    )
    return (new_max, totals, accumulated)


def empty_state(head_count, row_count):
    return (
        jnp.full((head_count, row_count), low_score, jnp.float32),
        jnp.zeros((head_count, row_count), jnp.float32),
        jnp.zeros((head_count, row_count, HD), jnp.float32),
    )


def visit_block(carry_state, packed, source, query_heads, query_clip, context):
    clip_ends, page_table, page_count, block_total = context
    row_count = query_heads.shape[0]
    head_count = query_heads.shape[1]
    allowed = allowed_keys(
        query_clip, source, clip_ends, page_table, page_count, block_total, row_count
    )
    key_heads = packed[0].reshape(-1, head_count, HD)
    value_heads = packed[1].reshape(-1, head_count, HD)
    return attend(carry_state, query_heads, key_heads, value_heads, allowed)


def gather_weight(out_weight, sizes, is_first):
    n_y, n_zl = sizes["y"], sizes["zl"]
    rows, cols = out_weight.shape
    other = swap_cores(out_weight)
    pair = jnp.where(
        is_first,
        jnp.concatenate([out_weight, other], axis=0),
        jnp.concatenate([other, out_weight], axis=0),
    )
    zl = lax.axis_index("zl")
    row_block = jnp.zeros((n_zl, 2 * rows, cols), out_weight.dtype)
    row_block = lax.dynamic_update_index_in_dim(row_block, pair, zl, 0)
    for d in range(1, n_zl):
        got = shifted(pair, "zl", n_zl, d, wrap=True)
        row_block = lax.dynamic_update_index_in_dim(row_block, got, (zl - d) % n_zl, 0)
    return row_block.reshape(n_zl * 2 * rows, cols)


def spread_weight(row_block, sizes, is_first):
    n_y = sizes["y"]
    y = lax.axis_index("y")
    cols = row_block.shape[1]
    full = jnp.zeros((n_y,) + row_block.shape, row_block.dtype)
    full = lax.dynamic_update_index_in_dim(full, row_block, y, 0)
    below_count = n_y // 2
    above_count = (n_y - 1) // 2
    received = []
    for j in range(1, below_count + 1):
        route = [(yy * 2, ((yy + j) % n_y) * 2) for yy in range(n_y)]
        if j <= above_count:
            route += [(yy * 2 + 1, ((yy - j) % n_y) * 2 + 1) for yy in range(n_y)]
        received.append(lax.ppermute(row_block, ("y", "c"), route))
    traded = swap_cores(jnp.stack(received))
    for j in range(1, below_count + 1):
        got = received[j - 1]
        if j <= above_count:
            here = jnp.where(is_first, (y - j) % n_y, (y + j) % n_y)
            there = jnp.where(is_first, (y + j) % n_y, (y - j) % n_y)
            full = lax.dynamic_update_index_in_dim(full, got, here, 0)
            full = lax.dynamic_update_index_in_dim(full, traded[j - 1], there, 0)
        else:
            value = jnp.where(is_first, got, traded[j - 1])
            full = lax.dynamic_update_index_in_dim(full, value, (y - j) % n_y, 0)
    return full.reshape(n_y * row_block.shape[0], cols)


def gather_attention(attention_local, sizes):
    n_x = sizes["x"]
    n_tensor = sizes["zh"] * n_x
    row_count, width = attention_local.shape
    zh = lax.axis_index("zh")
    x = lax.axis_index("x")
    partner = lax.ppermute(attention_local, "zh", [(0, 1), (1, 0)])
    both = jnp.where(
        zh == 0,
        jnp.concatenate([attention_local, partner], axis=1),
        jnp.concatenate([partner, attention_local], axis=1),
    )
    pieces = [(both, x)]
    for d in range(1, n_x):
        pieces.append((shifted(both, "x", n_x, d, wrap=True), (x - d) % n_x))
    full = jnp.zeros((row_count, n_tensor * width), attention_local.dtype)
    for piece, piece_x in pieces:
        for half in range(2):
            start = pl_multiple((half * n_x + piece_x) * width)
            full = lax.dynamic_update_slice(
                full, piece[:, half * width:(half + 1) * width], (jnp.int32(0), start)
            )
    return full


def pl_multiple(value):
    return value.astype(jnp.int32)


def make_local(sizes):
    n_chip = sizes["y"] * sizes["zl"]

    def local(
        queries,
        key_tiles,
        value_tiles,
        cache_keys,
        cache_values,
        hidden,
        out_weight,
        gate_table,
        lengths,
        page_table,
        page_count,
        timestep,
    ):
        row_count = queries.shape[0]
        tile_width = queries.shape[1]
        head_count = tile_width // HD
        block_total = n_chip * 2
        chip = lax.axis_index("y") * sizes["zl"] + lax.axis_index("zl")
        core = lax.axis_index("c")
        is_first = core == 0
        seq_index = chip * 2 + core
        clip_ends = jnp.cumsum(lengths, dtype=jnp.int32)
        row_ids = jnp.arange(row_count, dtype=jnp.int32)
        positions = seq_index * row_count + row_ids
        query_clip = clip_index(positions, clip_ends)
        query_heads = queries.reshape(row_count, head_count, HD)
        context = (clip_ends, page_table, page_count, block_total)
        packed = jnp.stack(
            [
                jnp.concatenate([key_tiles, cache_keys.reshape(-1, tile_width)], axis=0),
                jnp.concatenate([value_tiles, cache_values.reshape(-1, tile_width)], axis=0),
            ]
        )
        sign = 1 - 2 * core
        own_pair = swap_cores(packed)
        row_block = gather_weight(out_weight, sizes, is_first)
        packed, row_block, own_pair = lax.optimization_barrier((packed, row_block, own_pair))

        carry_state = visit_block(
            empty_state(head_count, row_count), packed, seq_index, query_heads, query_clip, context
        )
        carry_state = visit_block(
            carry_state, own_pair, seq_index + sign, query_heads, query_clip, context
        )
        above = {}
        below = {}
        for d in range(1, 4):
            above[d] = shifted(packed, CHIP, n_chip, -d)
            carry_state = visit_block(
                carry_state, above[d], seq_index + 2 * d, query_heads, query_clip, context
            )
            below[d] = shifted(packed, CHIP, n_chip, d)
            carry_state = visit_block(
                carry_state, below[d], seq_index - 2 * d, query_heads, query_clip, context
            )
        row_block, above[3], below[3] = lax.optimization_barrier((row_block, above[3], below[3]))
        weight_full = spread_weight(row_block, sizes, is_first)
        selected = jnp.where(
            is_first,
            jnp.stack([above[1], above[2], above[3], below[1], below[2]]),
            jnp.stack([below[1], below[2], below[3], above[1], above[2]]),
        )
        traded = swap_cores(selected)
        for slot, offset in enumerate((-1, -3, -5, 3, 5)):
            carry_state = visit_block(
                carry_state, traded[slot], seq_index + sign * offset, query_heads, query_clip, context
            )
        running_max, totals, accumulated = carry_state
        result = accumulated / totals[:, :, None]
        attention_local = (
            jnp.transpose(result, (1, 0, 2)).reshape(row_count, tile_width).astype(jnp.bfloat16)
        )
        attention = gather_attention(attention_local, sizes)
        projected = jnp.dot(attention, weight_full, preferred_element_type=jnp.float32)
        clip_total = lengths.shape[0]
        step_onehot = (
            timestep[:, None] == jnp.arange(gate_table.shape[0], dtype=jnp.int32)[None, :]
        ).astype(jnp.float32)
        clip_gate = jnp.dot(
            step_onehot, gate_table, precision=lax.Precision.HIGHEST, preferred_element_type=jnp.float32
        )
        clip_onehot = (
            query_clip[:, None] == jnp.arange(clip_total, dtype=jnp.int32)[None, :]
        ).astype(jnp.float32)
        token_gate = jnp.dot(
            clip_onehot, clip_gate, precision=lax.Precision.HIGHEST, preferred_element_type=jnp.float32
        )
        return (hidden.astype(jnp.float32) + token_gate * projected).astype(jnp.bfloat16)

    return local


def solution(mesh):
    n_seq = mesh.shape["seq"]
    n_tensor = mesh.shape["tensor"]
    sizes = {"y": n_seq // 8, "zl": 4, "c": 2, "zh": 2, "x": n_tensor // 2}
    devices = np.asarray(mesh.devices).reshape(tuple(sizes[a] for a in AXES))
    fine = Mesh(devices, AXES)
    return jax.shard_map(
        make_local(sizes),
        mesh=fine,
        in_specs=(
            P(SEQ, TENSOR),
            P(SEQ, TENSOR),
            P(SEQ, TENSOR),
            P(SEQ, None, TENSOR),
            P(SEQ, None, TENSOR),
            P(SEQ, TENSOR),
            P(SEQ, TENSOR),
            P(None, TENSOR),
            P(),
            P(),
            P(),
            P(),
        ),
        out_specs=P(SEQ, TENSOR),
        check_vma=False,
    )
```

```python
import math

import numpy as np
import jax
import jax.numpy as jnp
from jax import lax
from jax.sharding import Mesh, PartitionSpec as P

HD = 128
PAGE = 128
POOL = 2
REACH = 6

AXES = ("y", "zl", "c", "zh", "x")
SEQ = ("y", "zl", "c")
TENSOR = ("zh", "x")
CHIP = ("y", "zl")

low_score = -1e30


def shifted(block, axes, size, distance, wrap=False):
    if wrap:
        route = [(i, (i + distance) % size) for i in range(size)]
    else:
        route = [(i, i + distance) for i in range(size) if 0 <= i + distance < size]
    return lax.ppermute(block, axes, route)


def swap_cores(block):
    return lax.ppermute(block, "c", [(0, 1), (1, 0)])


def clip_index(positions, clip_ends):
    return jnp.sum((positions[:, None] >= clip_ends[None, :]).astype(jnp.int32), axis=1)


def allowed_keys(query_clip, source, clip_ends, page_table, page_count, block_total, row_count):
    key_pos = source * row_count + jnp.arange(row_count, dtype=jnp.int32)
    in_range = (source >= 0) & (source < block_total)
    same_clip = (query_clip[:, None] == clip_index(key_pos, clip_ends)[None, :]) & in_range
    clip_total = clip_ends.shape[0]
    page_ids = source * POOL + jnp.arange(POOL, dtype=jnp.int32)
    live_slots = jnp.arange(page_table.shape[1], dtype=jnp.int32)[None, :] < page_count[:, None]
    named_pages = jnp.any(
        live_slots[:, :, None] & (page_table[:, :, None] == page_ids[None, None, :]), axis=1
    )
    member = query_clip[:, None] == jnp.arange(clip_total, dtype=jnp.int32)[None, :]
    page_ok = jnp.any(member[:, :, None] & named_pages[None], axis=1) & in_range
    page_ok = jnp.repeat(page_ok, PAGE, axis=1)
    return jnp.concatenate([same_clip, page_ok], axis=1)


def attend(carry_state, query_heads, key_heads, value_heads, allowed):
    running_max, totals, accumulated = carry_state
    scores = jnp.einsum(
        "qhd,khd->hqk", query_heads, key_heads, preferred_element_type=jnp.float32
    ) * (1.0 / math.sqrt(HD))
    scores = jnp.where(allowed[None], scores, low_score)
    new_max = jnp.maximum(running_max, jnp.max(scores, axis=2))
    factor = jnp.exp(running_max - new_max)
    weights = jnp.where(allowed[None], jnp.exp(scores - new_max[:, :, None]), 0.0)
    totals = totals * factor + jnp.sum(weights, axis=2)
    accumulated = accumulated * factor[:, :, None] + jnp.einsum(
        "hqk,khd->hqd",
        weights.astype(jnp.bfloat16),
        value_heads,
        preferred_element_type=jnp.float32,
    )
    return (new_max, totals, accumulated)


def empty_state(head_count, row_count):
    return (
        jnp.full((head_count, row_count), low_score, jnp.float32),
        jnp.zeros((head_count, row_count), jnp.float32),
        jnp.zeros((head_count, row_count, HD), jnp.float32),
    )


def visit_block(carry_state, packed, source, query_heads, query_clip, context):
    clip_ends, page_table, page_count, block_total = context
    row_count = query_heads.shape[0]
    head_count = query_heads.shape[1]
    allowed = allowed_keys(
        query_clip, source, clip_ends, page_table, page_count, block_total, row_count
    )
    key_heads = packed[0].reshape(-1, head_count, HD)
    value_heads = packed[1].reshape(-1, head_count, HD)
    return attend(carry_state, query_heads, key_heads, value_heads, allowed)


def gather_weight(out_weight, sizes, is_first):
    n_y, n_zl = sizes["y"], sizes["zl"]
    rows, cols = out_weight.shape
    other = swap_cores(out_weight)
    pair = jnp.where(
        is_first,
        jnp.concatenate([out_weight, other], axis=0),
        jnp.concatenate([other, out_weight], axis=0),
    )
    zl = lax.axis_index("zl")
    row_block = jnp.zeros((n_zl, 2 * rows, cols), out_weight.dtype)
    row_block = lax.dynamic_update_index_in_dim(row_block, pair, zl, 0)
    for d in range(1, n_zl):
        got = shifted(pair, "zl", n_zl, d, wrap=True)
        row_block = lax.dynamic_update_index_in_dim(row_block, got, (zl - d) % n_zl, 0)
    return row_block.reshape(n_zl * 2 * rows, cols)


def spread_weight(row_block, sizes, is_first):
    n_y = sizes["y"]
    y = lax.axis_index("y")
    cols = row_block.shape[1]
    full = jnp.zeros((n_y,) + row_block.shape, row_block.dtype)
    full = lax.dynamic_update_index_in_dim(full, row_block, y, 0)
    below_count = n_y // 2
    above_count = (n_y - 1) // 2
    received = []
    for j in range(1, below_count + 1):
        route = [(yy * 2, ((yy + j) % n_y) * 2) for yy in range(n_y)]
        if j <= above_count:
            route += [(yy * 2 + 1, ((yy - j) % n_y) * 2 + 1) for yy in range(n_y)]
        received.append(lax.ppermute(row_block, ("y", "c"), route))
    traded = swap_cores(jnp.stack(received))
    for j in range(1, below_count + 1):
        got = received[j - 1]
        if j <= above_count:
            here = jnp.where(is_first, (y - j) % n_y, (y + j) % n_y)
            there = jnp.where(is_first, (y + j) % n_y, (y - j) % n_y)
            full = lax.dynamic_update_index_in_dim(full, got, here, 0)
            full = lax.dynamic_update_index_in_dim(full, traded[j - 1], there, 0)
        else:
            value = jnp.where(is_first, got, traded[j - 1])
            full = lax.dynamic_update_index_in_dim(full, value, (y - j) % n_y, 0)
    return full.reshape(n_y * row_block.shape[0], cols)


def gather_attention(attention_local, sizes):
    n_x = sizes["x"]
    n_tensor = sizes["zh"] * n_x
    row_count, width = attention_local.shape
    zh = lax.axis_index("zh")
    x = lax.axis_index("x")
    partner = lax.ppermute(attention_local, "zh", [(0, 1), (1, 0)])
    both = jnp.where(
        zh == 0,
        jnp.concatenate([attention_local, partner], axis=1),
        jnp.concatenate([partner, attention_local], axis=1),
    )
    pieces = [(both, x)]
    for d in range(1, n_x):
        pieces.append((shifted(both, "x", n_x, d, wrap=True), (x - d) % n_x))
    full = jnp.zeros((row_count, n_tensor * width), attention_local.dtype)
    for piece, piece_x in pieces:
        for half in range(2):
            start = pl_multiple((half * n_x + piece_x) * width)
            full = lax.dynamic_update_slice(
                full, piece[:, half * width:(half + 1) * width], (jnp.int32(0), start)
            )
    return full


def pl_multiple(value):
    return value.astype(jnp.int32)


def make_local(sizes):
    n_chip = sizes["y"] * sizes["zl"]

    def local(
        queries,
        key_tiles,
        value_tiles,
        cache_keys,
        cache_values,
        hidden,
        out_weight,
        gate_table,
        lengths,
        page_table,
        page_count,
        timestep,
    ):
        row_count = queries.shape[0]
        tile_width = queries.shape[1]
        head_count = tile_width // HD
        block_total = n_chip * 2
        chip = lax.axis_index("y") * sizes["zl"] + lax.axis_index("zl")
        core = lax.axis_index("c")
        is_first = core == 0
        seq_index = chip * 2 + core
        clip_ends = jnp.cumsum(lengths, dtype=jnp.int32)
        row_ids = jnp.arange(row_count, dtype=jnp.int32)
        positions = seq_index * row_count + row_ids
        query_clip = clip_index(positions, clip_ends)
        query_heads = queries.reshape(row_count, head_count, HD)
        context = (clip_ends, page_table, page_count, block_total)
        packed = jnp.stack(
            [
                jnp.concatenate([key_tiles, cache_keys.reshape(-1, tile_width)], axis=0),
                jnp.concatenate([value_tiles, cache_values.reshape(-1, tile_width)], axis=0),
            ]
        )
        sign = 1 - 2 * core
        own_pair = swap_cores(packed)
        row_block = gather_weight(out_weight, sizes, is_first)
        carry_state = visit_block(
            empty_state(head_count, row_count), packed, seq_index, query_heads, query_clip, context
        )
        carry_state = visit_block(
            carry_state, own_pair, seq_index + sign, query_heads, query_clip, context
        )
        packed, row_block, carry_state = lax.optimization_barrier((packed, row_block, carry_state))
        weight_full = spread_weight(row_block, sizes, is_first)
        above = {}
        below = {}
        for d in range(1, 4):
            above[d] = shifted(packed, CHIP, n_chip, -d)
            carry_state = visit_block(
                carry_state, above[d], seq_index + 2 * d, query_heads, query_clip, context
            )
            below[d] = shifted(packed, CHIP, n_chip, d)
            carry_state = visit_block(
                carry_state, below[d], seq_index - 2 * d, query_heads, query_clip, context
            )
        selected = jnp.where(
            is_first,
            jnp.stack([above[1], above[2], above[3], below[1], below[2]]),
            jnp.stack([below[1], below[2], below[3], above[1], above[2]]),
        )
        traded = swap_cores(selected)
        for slot, offset in enumerate((-1, -3, -5, 3, 5)):
            carry_state = visit_block(
                carry_state, traded[slot], seq_index + sign * offset, query_heads, query_clip, context
            )
        running_max, totals, accumulated = carry_state
        result = accumulated / totals[:, :, None]
        attention_local = (
            jnp.transpose(result, (1, 0, 2)).reshape(row_count, tile_width).astype(jnp.bfloat16)
        )
        attention = gather_attention(attention_local, sizes)
        projected = jnp.dot(attention, weight_full, preferred_element_type=jnp.float32)
        clip_total = lengths.shape[0]
        step_onehot = (
            timestep[:, None] == jnp.arange(gate_table.shape[0], dtype=jnp.int32)[None, :]
        ).astype(jnp.float32)
        clip_gate = jnp.dot(
            step_onehot, gate_table, precision=lax.Precision.HIGHEST, preferred_element_type=jnp.float32
        )
        clip_onehot = (
            query_clip[:, None] == jnp.arange(clip_total, dtype=jnp.int32)[None, :]
        ).astype(jnp.float32)
        token_gate = jnp.dot(
            clip_onehot, clip_gate, precision=lax.Precision.HIGHEST, preferred_element_type=jnp.float32
        )
        return (hidden.astype(jnp.float32) + token_gate * projected).astype(jnp.bfloat16)

    return local


def solution(mesh):
    n_seq = mesh.shape["seq"]
    n_tensor = mesh.shape["tensor"]
    sizes = {"y": n_seq // 8, "zl": 4, "c": 2, "zh": 2, "x": n_tensor // 2}
    devices = np.asarray(mesh.devices).reshape(tuple(sizes[a] for a in AXES))
    fine = Mesh(devices, AXES)
    return jax.shard_map(
        make_local(sizes),
        mesh=fine,
        in_specs=(
            P(SEQ, TENSOR),
            P(SEQ, TENSOR),
            P(SEQ, TENSOR),
            P(SEQ, None, TENSOR),
            P(SEQ, None, TENSOR),
            P(SEQ, TENSOR),
            P(SEQ, TENSOR),
            P(None, TENSOR),
            P(),
            P(),
            P(),
            P(),
        ),
        out_specs=P(SEQ, TENSOR),
        check_vma=False,
    )
```
